32 devices in a mesh: ap: 8 (over z, y), sc: 4 (over x, core).
Axes of the slice: x: 2, y: 2, z: 4, core: 2. Of those that a mesh axis runs over, the one named last changes fastest.
Arguments:
- pilot_received: bfloat16 [4, 16, 4, 1024], P('sc', None, None, 'ap'), may hold values from -6 to 6
- received: bfloat16 [4, 4, 1024, 128], P('sc', None, 'ap'), may hold values from -6 to 6
- large_scale: bfloat16 [96, 1024], P(None, 'ap'), may hold values from 0.049804688 to 1
- pilot_index: int32 [96], replicated, may hold values from 0 to 15
- serving: int32 [1024, 32], P('ap'), may hold values from 0 to 95, all different within a row
- user_group: int32 [96], replicated, may hold values from 0 to 1, as said below
Outputs:
- estimates: float32 [128, 4, 128], P('ap', 'sc')
The draws below stay inside these ranges and needn't reach their ends.
Inputs may be any that keep to these rules, and one draw needn't show every extreme that they name: `user_group`: at most 64 users share a group, and some group has exactly 64 users. `serving`: each access point's list names 32 different users, and every user is named by some list.
All inputs are finite; a program needn't handle non-finite values.
Results may differ from the reference program's by a relative error of at most 0.0025.
The reference program's roundings to bfloat16 on the way count: a program that leaves them out, or rounds other values in their place, can miss the bound.
Values may be sent and summed in bfloat16 or wider, within the bound.
A program may use at most 64 MiB of HBM per device.

```python
import math
import jax
import jax.numpy as jnp
from jax import lax

AP_ANTENNA_COUNT = 4
GROUP_SLOTS = 64
PILOT_COUNT = 16
SERVED_USERS = 32
DATA_SYMBOLS = 128
N_OWN = 2
USER_COUNT = 96
ACCESS_POINTS = 1024
SUBCARRIER_BLOCKS = 4


def draw_user_group(key, part):
    first_key, second_key, third_key = jax.random.split(key, 3)
    pairs = N_OWN // 2
    base_size = 3 * GROUP_SLOTS // 4
    deficit = jax.random.randint(first_key, (pairs,), GROUP_SLOTS // 8, GROUP_SLOTS // 4 + 1)
    deficit = deficit.at[0].set(GROUP_SLOTS // 4)
    sizes = jnp.stack([base_size + deficit, base_size - deficit], axis=1).reshape(N_OWN)
    labels = jax.random.permutation(second_key, N_OWN).astype(jnp.int32)
    ends = jnp.cumsum(sizes)
    positions = jnp.arange(USER_COUNT, dtype=jnp.int32)
    which = jnp.sum((positions[:, None] >= ends[None, :]).astype(jnp.int32), axis=1)
    label_of_position = labels[which]
    shuffle = jax.random.permutation(third_key, USER_COUNT)
    return jnp.zeros((USER_COUNT,), jnp.int32).at[shuffle].set(label_of_position)


def set_ends(array, key, low, top_value):
    place = [jax.random.randint(jax.random.fold_in(key, axis), (), 0, length) for axis, length in enumerate(array.shape)]
    widest = array.shape.index(max(array.shape))
    neighbour = place[:widest] + [(place[widest] + 1) % array.shape[widest]] + place[widest + 1:]
    return array.at[tuple(place)].set(low).at[tuple(neighbour)].set(top_value)


def level_of(key, dims, shards, smallest, high):
    def one(position, blocks):
        draws = jax.random.uniform(jax.random.fold_in(jax.random.fold_in(key, 6), position), (blocks,), jnp.float32, smallest / len(shards), high / len(shards))
        return jnp.repeat(jnp.exp(draws), dims[position] // blocks).reshape((-1,) + (1,) * (len(dims) - position - 1))

    loudness = one(*shards[0])
    for cut in shards[1:]:
        loudness = loudness * one(*cut)
    return loudness


def distinct(own_key, rows, amount, top, lift):
    order = jax.random.permutation(jax.random.fold_in(own_key, 1), amount)
    pull = order
    for power in range(3):
        pull = pull * pull // amount
    pull = pull * lift // amount
    lots = jax.random.randint(jax.random.fold_in(own_key, 2), (rows, amount), 0, 4096) + pull
    fixed_rows = jax.random.permutation(jax.random.fold_in(own_key, 3), rows)[jnp.arange(amount) % rows]
    lots = jnp.where(jnp.arange(rows)[:, None] == fixed_rows[None, :], 1 << 14, lots)
    score = lots * amount + jnp.arange(amount)
    return lax.top_k(score.astype(jnp.int32), top)[1].astype(jnp.int32)


def bell_draw(stream_key, extent, scale, bound, cuts=(), kind=jnp.bfloat16):
    values = scale * jax.random.normal(stream_key, extent, jnp.float32)
    if cuts:
        values = values * level_of(stream_key, extent, cuts, -0.22, 0.18)
    return jnp.clip(values, -bound, bound).astype(kind)


def setup_inputs(seed: int = 0) -> dict:
    arg_keys = jax.random.split(jax.random.key(seed), 7)
    pilot_received = bell_draw(arg_keys[0], (SUBCARRIER_BLOCKS, PILOT_COUNT, AP_ANTENNA_COUNT, ACCESS_POINTS), 1.0, 6.0, ((0, 4), (3, 8)))
    received = bell_draw(arg_keys[1], (SUBCARRIER_BLOCKS, AP_ANTENNA_COUNT, ACCESS_POINTS, DATA_SYMBOLS), 1.0, 6.0, ((0, 4), (2, 8)))
    large_scale = jnp.clip(jnp.exp(math.log(1.0) - 2.9996462 * jax.random.uniform(arg_keys[2], (USER_COUNT, ACCESS_POINTS), jnp.float32) ** level_of(arg_keys[2], (USER_COUNT, ACCESS_POINTS), ((1, 8),), -0.2, 0.2)), 0.049804688, 1.0).astype(jnp.bfloat16)
    pilot_index = set_ends(jax.random.randint(arg_keys[3], (USER_COUNT,), 0, PILOT_COUNT), jax.random.fold_in(arg_keys[3], 1), 0, PILOT_COUNT - 1).astype(jnp.int32)
    serving = distinct(arg_keys[4], ACCESS_POINTS, USER_COUNT, SERVED_USERS, 0)
    user_group = draw_user_group(jax.random.fold_in(arg_keys[6], 71), 0)
    return {"pilot_received": pilot_received, "received": received, "large_scale": large_scale, "pilot_index": pilot_index, "serving": serving, "user_group": user_group}


NOISE_LEVEL = 0.05

def slot_tables(pilot_index, user_group, group_count):
    labels = jnp.arange(group_count, dtype=jnp.int32)
    group_hot = (user_group[:, None] == labels[None, :]).astype(jnp.int32)
    ranks_in = lax.optimization_barrier(jnp.sum(jnp.cumsum(group_hot, axis=0) * group_hot, axis=1)) - 1
    slot_ids = (user_group * GROUP_SLOTS + ranks_in).astype(jnp.int32)
    members = jnp.zeros((group_count * GROUP_SLOTS,), jnp.int32).at[slot_ids].set(jnp.arange(user_group.shape[0], dtype=jnp.int32))
    occupied = jnp.zeros((group_count * GROUP_SLOTS,), jnp.float32).at[slot_ids].set(1.0)
    slot_pilot = pilot_index[members]
    return (members, occupied, slot_pilot)

def inverse_columns(factor, columns):
    first = lax.linalg.triangular_solve(factor, columns, left_side=True, lower=True)
    return lax.linalg.triangular_solve(factor, first, left_side=True, lower=True, transpose_a=True)

def reference(pilot_received, received, large_scale, pilot_index, serving, user_group):
    members, occupied, slot_pilot = slot_tables(pilot_index, user_group, N_OWN)
    pilots = pilot_received.astype(jnp.float32)
    before = jnp.concatenate([pilots[:1], pilots[:-1]], axis=0)
    after = jnp.concatenate([pilots[1:], pilots[-1:]], axis=0)
    smooth = 0.25 * before + 0.5 * pilots + 0.25 * after
    pilot_hot = (pilot_index[None, :] == jnp.arange(PILOT_COUNT, dtype=jnp.int32)[:, None]).astype(jnp.bfloat16)
    contamination = 1.0 + PILOT_COUNT / USER_COUNT * jnp.dot(pilot_hot.astype(jnp.float32), large_scale.astype(jnp.float32), preferred_element_type=jnp.float32)
    serve_mask = jnp.zeros((USER_COUNT, ACCESS_POINTS), jnp.bfloat16).at[serving, jnp.arange(ACCESS_POINTS, dtype=jnp.int32)[:, None]].set(1.0)
    gramian_scale = 1.0 / (AP_ANTENNA_COUNT * ACCESS_POINTS)
    estimator_scale = 1.0 / math.sqrt(AP_ANTENNA_COUNT * ACCESS_POINTS * SERVED_USERS / USER_COUNT)
    data_signal = received.astype(jnp.float32).reshape(SUBCARRIER_BLOCKS, AP_ANTENNA_COUNT * ACCESS_POINTS, DATA_SYMBOLS)
    identity = jnp.eye(GROUP_SLOTS, dtype=jnp.float32)

    def one_group(group):
        start = (group * GROUP_SLOTS).astype(jnp.int32)
        member_rows = lax.dynamic_slice_in_dim(members, start, GROUP_SLOTS)
        occupied_rows = lax.dynamic_slice_in_dim(occupied, start, GROUP_SLOTS)
        pilot_rows = lax.dynamic_slice_in_dim(slot_pilot, start, GROUP_SLOTS)
        coeff = occupied_rows[:, None] * large_scale[member_rows].astype(jnp.float32) * lax.rsqrt(contamination[pilot_rows])
        channel_gain = (smooth[:, pilot_rows] * coeff[None, :, None, :]).astype(jnp.bfloat16)
        flattened = channel_gain.reshape(SUBCARRIER_BLOCKS, GROUP_SLOTS, AP_ANTENNA_COUNT * ACCESS_POINTS).astype(jnp.float32)
        gram = jnp.einsum('bgx,bhx->bgh', flattened, flattened) * gramian_scale
        system = gram + NOISE_LEVEL * identity
        factor = jnp.linalg.cholesky(system)
        inverse = inverse_columns(factor, jnp.broadcast_to(identity, system.shape))
        weights = jnp.swapaxes(inverse, 1, 2).astype(jnp.bfloat16)
        combiner_weight = jnp.einsum('bkj,bjx->bkx', weights.astype(jnp.float32), flattened).astype(jnp.bfloat16)
        row_mask_values = serve_mask[member_rows] * occupied_rows[:, None].astype(jnp.bfloat16)
        masked_values = combiner_weight.reshape(SUBCARRIER_BLOCKS, GROUP_SLOTS, AP_ANTENNA_COUNT, ACCESS_POINTS) * row_mask_values[None, :, None, :]
        flattened_masked = masked_values.reshape(SUBCARRIER_BLOCKS, GROUP_SLOTS, AP_ANTENNA_COUNT * ACCESS_POINTS).astype(jnp.float32)
        return jnp.einsum('bsx,bxt->sbt', flattened_masked, data_signal) * estimator_scale
    result = lax.map(one_group, jnp.arange(N_OWN, dtype=jnp.int32))
    return result.reshape(N_OWN * GROUP_SLOTS, SUBCARRIER_BLOCKS, DATA_SYMBOLS)
```

```python
import functools
import math

import jax
import jax.numpy as jnp
from jax import lax
from jax.experimental import pallas as pl
from jax.experimental.pallas import tpu as pltpu
from jax.sharding import PartitionSpec as P

GROUP_SLOTS = 64


NOISE_LEVEL = 0.05


def extended_2(block, sides, width):
    for axis, dim in sides:
        count = lax.axis_size(axis)
        forward = [(i, i + 1) for i in range(count - 1)]
        backward = [(target, source) for source, target in forward]
        low = lax.ppermute(
            lax.slice_in_dim(block, block.shape[dim] - width, None, axis=dim), axis, forward
        )
        high = lax.ppermute(lax.slice_in_dim(block, 0, width, axis=dim), axis, backward)
        block = jnp.concatenate([low, block, high], axis=dim)
    return block


def slot_tables(pilot_index, user_group, group_count):
    labels = jnp.arange(group_count, dtype=jnp.int32)
    group_hot = (user_group[:, None] == labels[None, :]).astype(jnp.int32)
    users = jnp.arange(user_group.shape[0], dtype=jnp.int32)
    up_to = (users[:, None] >= users[None, :]).astype(jnp.bfloat16)
    counts = jnp.dot(up_to, group_hot.astype(jnp.bfloat16), preferred_element_type=jnp.float32)
    ranks_in = jnp.sum(counts.astype(jnp.int32) * group_hot, axis=1) - 1
    slot_ids = user_group * GROUP_SLOTS + ranks_in
    members = (
        jnp.zeros((group_count * GROUP_SLOTS,), jnp.int32)
        .at[slot_ids]
        .set(jnp.arange(user_group.shape[0], dtype=jnp.int32))
    )
    occupied = jnp.zeros((group_count * GROUP_SLOTS,), jnp.float32).at[slot_ids].set(1.0)
    slot_pilot = pilot_index[members]
    return (members, occupied, slot_pilot)


def inverse_columns(factor, columns):
    first = lax.linalg.triangular_solve(factor, columns, left_side=True, lower=True)
    return lax.linalg.triangular_solve(factor, first, left_side=True, lower=True, transpose_a=True)


def on_device(pilot_received, received, large_scale, pilot_index, serving, user_group):
    ap_count = lax.axis_size("ap")
    sc_count = lax.axis_size("sc")
    ap_index = lax.axis_index("ap")
    sc_index = lax.axis_index("sc")
    blocks_dev, tau_count, antennas, aps_dev = pilot_received.shape
    symbols = received.shape[3]
    users = pilot_index.shape[0]
    serve_count = serving.shape[1]
    groups = ap_count // 4
    quarter = GROUP_SLOTS // 4
    aps_total = aps_dev * ap_count
    members, occupied, slot_pilot = slot_tables(pilot_index, user_group, groups)
    extended = extended_2(pilot_received, (("sc", 0),), 1)
    block_ids = sc_index * blocks_dev + jnp.arange(blocks_dev, dtype=jnp.int32)
    first_block = (block_ids == 0)[:, None, None, None]
    final_block = (block_ids == blocks_dev * sc_count - 1)[:, None, None, None]
    middle = extended[1:-1].astype(jnp.float32)
    before = jnp.where(first_block, middle, extended[:-2].astype(jnp.float32))
    after = jnp.where(final_block, middle, extended[2:].astype(jnp.float32))
    smooth = 0.25 * before + 0.5 * middle + 0.25 * after
    pilot_hot = (pilot_index[None, :] == jnp.arange(tau_count, dtype=jnp.int32)[:, None]).astype(
        jnp.bfloat16
    )
    contamination = 1.0 + tau_count / users * jnp.dot(
        pilot_hot, large_scale, preferred_element_type=jnp.float32
    )
    serve_mask = (
        jnp.zeros((users, aps_dev), jnp.bfloat16)
        .at[serving, jnp.arange(aps_dev, dtype=jnp.int32)[:, None]]
        .set(1.0)
    )
    batch_groups = min(8, groups)
    batches = groups // batch_groups
    batch_rows = batch_groups * GROUP_SLOTS
    member_blocks = members.reshape(batches, batch_rows)
    occupied_blocks = occupied.reshape(batches, batch_rows)
    pilot_blocks = slot_pilot.reshape(batches, batch_rows)
    gramian_scale = 1.0 / (antennas * aps_total)

    def gram_batch(inputs):
        member_rows, occupied_rows, pilot_rows = inputs
        coeff = (
            occupied_rows[:, None]
            * large_scale[member_rows].astype(jnp.float32)
            * lax.rsqrt(contamination[pilot_rows])
        )
        row_hot = (pilot_rows[:, None] == jnp.arange(tau_count, dtype=jnp.int32)).astype(jnp.float32)
        picked = jnp.einsum("st,btnl->bsnl", row_hot, smooth, precision=lax.Precision.HIGHEST)
        channel_gain = (picked * coeff[None, :, None, :]).astype(jnp.bfloat16)
        channel_gain = channel_gain.reshape(
            blocks_dev, batch_groups, GROUP_SLOTS, antennas * aps_dev
        )
        gram = (
            jnp.einsum(
                "bogx,bohx->ogbh", channel_gain, channel_gain, preferred_element_type=jnp.float32
            )
            * gramian_scale
        )
        return (gram, channel_gain)

    partial_gram, channel_store = lax.map(
        gram_batch, (member_blocks, occupied_blocks, pilot_blocks)
    )
    partial_gram = partial_gram.reshape(groups * GROUP_SLOTS, blocks_dev, GROUP_SLOTS)
    summed = lax.psum(partial_gram, "ap")
    owned = lax.dynamic_slice_in_dim(summed, ap_index // 4 * GROUP_SLOTS, GROUP_SLOTS, 0)
    identity = jnp.eye(GROUP_SLOTS, dtype=jnp.float32)
    system = jnp.transpose(owned, (1, 0, 2)) + NOISE_LEVEL * identity
    factor = jnp.linalg.cholesky(system)
    columns = lax.dynamic_slice_in_dim(identity, ap_index % 4 * quarter, quarter, 1)
    solved = inverse_columns(factor, jnp.broadcast_to(columns, (blocks_dev, GROUP_SLOTS, quarter)))
    weight_rows = jnp.transpose(solved, (2, 0, 1)).astype(jnp.bfloat16)
    all_weights = lax.all_gather(weight_rows, "ap", axis=0, tiled=True)
    weight_blocks = all_weights.reshape(batches, batch_groups, GROUP_SLOTS, blocks_dev, GROUP_SLOTS)
    data_signal = received.reshape(blocks_dev, antennas * aps_dev, symbols)
    estimator_scale = 1.0 / math.sqrt(antennas * aps_total * serve_count / users)

    def estimate_batch(inputs):
        member_rows, occupied_rows, channel_gain, weights = inputs
        combiner_weight = jnp.einsum(
            "okbj,bojx->bokx", weights, channel_gain, preferred_element_type=jnp.float32
        ).astype(jnp.bfloat16)
        row_mask_values = serve_mask[member_rows] * occupied_rows[:, None].astype(jnp.bfloat16)
        masked_values = (
            combiner_weight.reshape(blocks_dev, batch_rows, antennas, aps_dev)
            * row_mask_values[None, :, None, :]
        )
        flattened_masked = masked_values.reshape(blocks_dev, batch_rows, antennas * aps_dev)
        return (
            jnp.einsum(
                "bsx,bxt->sbt", flattened_masked, data_signal, preferred_element_type=jnp.float32
            )
            * estimator_scale
        )

    terms = lax.map(estimate_batch, (member_blocks, occupied_blocks, channel_store, weight_blocks))
    terms = terms.reshape(groups * GROUP_SLOTS, blocks_dev, symbols)
    return lax.psum_scatter(terms, "ap", scatter_dimension=0, tiled=True)


LANES = 128
BF16 = jnp.bfloat16
F32 = jnp.float32
NT = (((1,), (1,)), ((), ()))


def iota(shape, dim):
    return lax.broadcasted_iota(jnp.int32, shape, dim)


def mm(a, b, dims=(((1,), (0,)), ((), ()))):
    return lax.dot_general(a, b, dims, preferred_element_type=F32)


def partners(me, n):
    found = []
    for flip in range(n - 1, 0, -1):
        peer = me
        for bit in (1 << b for b in range(n.bit_length() - 1)):
            if flip & bit:
                peer = peer + bit - 2 * bit * (me // bit % 2)
        found.append(peer)
    return found


def invert_pairs(mat, block=8):
    tile = 8
    inner = iota((tile, LANES), 1) % GROUP_SLOTS
    base = iota((tile, LANES), 1) - inner
    sub = iota((tile, LANES), 0)
    parts = [mat[i : i + tile] for i in range(0, GROUP_SLOTS, tile)]

    def line_of(part, line):
        return jnp.broadcast_to(part[line : line + 1], (tile, LANES))

    for start in range(0, GROUP_SLOTS, block):
        columns = [
            [jnp.take_along_axis(part, base + k, axis=1) for part in parts]
            for k in range(start, start + block)
        ]
        for j in range(0, block, 2):
            k = start + j
            home, line = divmod(k, tile)
            first, second = columns[j], columns[j + 1]
            p00, p01 = line_of(first[home], line), line_of(second[home], line)
            p11 = line_of(second[home], line + 1)
            scale = 1.0 / (p00 * p11 - p01 * p01)
            i00, i01, i11 = p11 * scale, -p01 * scale, p00 * scale

            def through(part):
                upper, lower = line_of(part, line), line_of(part, line + 1)
                return i00 * upper + i01 * lower, i01 * upper + i11 * lower

            def with_lines(part, upper, lower):
                return jnp.where(sub == line, upper, jnp.where(sub == line + 1, lower, part))

            for later in range(j + 2, block):
                ahead = columns[later]
                upper, lower = through(ahead[home])
                ahead = [a - c * upper - d * lower for a, c, d in zip(ahead, first, second)]
                ahead[home] = with_lines(ahead[home], upper, lower)
                columns[later] = ahead
            upper, lower = through(parts[home])
            upper = jnp.where(inner == k, -i00, jnp.where(inner == k + 1, -i01, upper))
            lower = jnp.where(inner == k, -i01, jnp.where(inner == k + 1, -i11, lower))
            pivots = inner // 2 == k // 2
            parts = [jnp.where(pivots, 0.0, p) - c * upper - d * lower for p, c, d in zip(parts, first, second)]
            parts[home] = with_lines(parts[home], upper, lower)
    return -jnp.concatenate(parts, axis=0)


def fused_kernel(
    n, sc_count, users, tau_count, antennas, gram_scale, estimate_scale,
    pilot_ref, data_ref, large_ref, pilot_index_ref, serving_ref, group_ref,
    out_ref,
    pilots, data, large_in, pilot_index, serving_in, group_in,
    gram_src, gram_recv, terms, term_recv,
    load, halo_send, halo_recv, gram_send, gram_arrive, out_send, out_recv, far_entered,
):
    me = lax.axis_index("ap")
    sc = lax.axis_index("sc")
    right, left = sc + 1, sc - 1
    peers = partners(me, n)
    slots = n // 4 * GROUP_SLOTS
    pilot_rows = tau_count * antennas
    gram_rows = GROUP_SLOTS // 2 + 1
    out_rows = slots // n

    barrier = pltpu.get_barrier_semaphore()
    near = peers[n // 2 - 1 :]
    for peer in near:
        pl.semaphore_signal(barrier, inc=1, device_id={"ap": peer}, device_id_type=pl.DeviceIdType.MESH)
    has_left, has_right = sc > 0, sc < sc_count - 1
    for present, neighbour in ((has_left, left), (has_right, right)):

        @pl.when(present)
        def _():
            pl.semaphore_signal(barrier, inc=1, device_id={"sc": neighbour}, device_id_type=pl.DeviceIdType.MESH)

    loads = []
    for source, target in (
        (group_ref, group_in), (pilot_index_ref, pilot_index), (large_ref, large_in), (serving_ref, serving_in),
        (pilot_ref, pilots.at[pl.ds(pilot_rows, pilot_rows)]), (data_ref, data),
    ):
        loads.append(pltpu.make_async_copy(source, target, load.at[len(loads)]))
        loads[-1].start()

    def make(src, dst, send_sem, recv_sem, where):
        return pltpu.make_async_remote_copy(
            src_ref=src, dst_ref=dst, send_sem=send_sem, recv_sem=recv_sem,
            device_id=where, device_id_type=pl.DeviceIdType.MESH,
        )

    def send(*parts):
        copy = make(*parts)
        copy.start()
        return copy

    for copy in loads[:4]:
        copy.wait()
    group_row = group_in[...]
    in_group = group_row == iota((8, users), 0)
    in_group = jnp.where(in_group, 1.0, 0.0)
    earlier = jnp.where(iota((users, users), 0) < iota((users, users), 1), 1.0, 0.0).astype(BF16)
    counts = mm(in_group.astype(BF16), earlier)
    ranks = jnp.sum(counts * in_group, axis=0, keepdims=True).astype(jnp.int32)
    slot_row = group_row * GROUP_SLOTS + ranks
    hot = jnp.where(iota((slots, users), 0) == slot_row, 1.0, 0.0)
    member = (
        jnp.sum(hot * (iota((slots, users), 1) + 1).astype(F32), axis=1, keepdims=True) - 1.0
    ).astype(jnp.int32)
    hot = hot.astype(BF16)
    pilot_hot = jnp.where(iota((tau_count, users), 0) == pilot_index[...], 1.0, 0.0).astype(BF16)
    slot_pilot = mm(hot, pilot_hot, NT).astype(BF16)
    same_pilot = mm(slot_pilot, pilot_hot).astype(BF16)
    large = large_in[...]
    contamination = 1.0 + tau_count / users * mm(same_pilot, large)
    coeff = mm(hot, large) * lax.rsqrt(contamination)

    low = jnp.where(sc == 0, 0.0, 0.25)
    high = jnp.where(sc == sc_count - 1, 0.0, 0.25)
    place = iota((tau_count, 3 * pilot_rows), 1)
    weight = jnp.where(place < pilot_rows, low, jnp.where(place < 2 * pilot_rows, 1.0 - low - high, high))
    pick = jnp.where(place % pilot_rows // antennas == iota(place.shape, 0), weight, 0.0)
    picked = mm(slot_pilot, pick.astype(BF16))
    antenna = iota(picked.shape, 1) % antennas
    spread = jnp.concatenate(
        [jnp.where(antenna == a, picked, 0.0).astype(BF16) for a in range(antennas)], axis=0
    )
    serving = serving_in[...]
    mask = jnp.zeros((slots, serving.shape[1]), F32)
    for j in range(serving.shape[0]):
        mask = jnp.where(member == serving[j : j + 1, :], 1.0, mask)
    mask = mask.astype(BF16)

    pl.semaphore_wait(barrier, n // 2 + has_left.astype(jnp.int32) + has_right.astype(jnp.int32))
    blank = jnp.zeros((pilot_rows, pilots.shape[1]), BF16)
    upward = make(pilot_ref, pilots.at[pl.ds(0, pilot_rows)], halo_send.at[0], halo_recv.at[0], {"sc": right})
    downward = make(pilot_ref, pilots.at[pl.ds(2 * pilot_rows, pilot_rows)], halo_send.at[1], halo_recv.at[1], {"sc": left})
    pl.when(has_right)(upward.start)
    pl.when(has_left)(downward.start)

    @pl.when(jnp.logical_not(has_left))
    def _():
        pilots[pl.ds(0, pilot_rows), :] = blank

    @pl.when(jnp.logical_not(has_right))
    def _():
        pilots[pl.ds(2 * pilot_rows, pilot_rows), :] = blank

    pl.semaphore_signal(far_entered, inc=1, device_id={"ap": near[0]}, device_id_type=pl.DeviceIdType.MESH)
    for copy in loads[4:]:
        copy.wait()
    pl.when(has_left)(upward.wait_recv)
    pl.when(has_right)(downward.wait_recv)
    smooth = mm(spread, pilots[...])
    channel = jnp.concatenate(
        [(smooth[a * slots : (a + 1) * slots] * coeff).astype(BF16) for a in range(antennas)], axis=1
    )
    gram = mm(channel, channel, NT) * gram_scale
    half = iota((GROUP_SLOTS, LANES), 1) < GROUP_SLOTS
    row, column = iota(half.shape, 0), iota(half.shape, 1) % GROUP_SLOTS
    own = jnp.where(half, column - row, row - column - 1) >= 0
    middle = GROUP_SLOTS // 2
    pair = jnp.where(half, gram[:GROUP_SLOTS], gram[GROUP_SLOTS:])
    packed = jnp.where(own, pair, pltpu.roll(pair, GROUP_SLOTS, 1))
    gram_src[pl.ds(0, middle), :] = jnp.where(half[:middle], packed[:middle], packed[middle:])
    gram_src[pl.ds(middle, 1), :] = jnp.sum(jnp.where(row == column, pair, 0.0), axis=0, keepdims=True)
    exchange = [None] * len(peers)
    far = len(peers) - len(near)
    for i in [*range(far, len(peers)), *range(far)]:
        if i == 0:
            pl.semaphore_wait(far_entered, 1)
        exchange[i] = send(
            gram_src.at[pl.ds(0, gram_rows)], gram_recv.at[i, pl.ds(0, gram_rows)],
            gram_send.at[i], gram_arrive.at[i], {"ap": peers[i]},
        )
    total = gram_src[pl.ds(0, gram_rows), :]
    for i, copy in reversed(list(enumerate(exchange))):
        copy.wait_recv()
        total = total + gram_recv[i, pl.ds(0, gram_rows), :]
    upper, diagonal = total[:middle], total[middle:gram_rows]
    other = pltpu.roll(upper, GROUP_SLOTS, 1)
    packed = jnp.concatenate(
        [jnp.where(half[:middle], upper, other), jnp.where(half[:middle], other, upper)], axis=0
    )
    mirrored = jnp.transpose(jnp.concatenate([packed, packed], axis=0))[:GROUP_SLOTS]
    system = jnp.where(own, packed, mirrored)
    system = jnp.where(row == column, diagonal + NOISE_LEVEL, system)
    inverse = invert_pairs(system)
    weights = jnp.concatenate(
        [jnp.where(half, inverse, 0.0), jnp.where(half, 0.0, inverse)], axis=0
    ).astype(BF16)
    combine = mm(weights, channel).astype(BF16)
    masked = combine * jnp.concatenate([mask] * antennas, axis=1)
    terms[...] = mm(masked, data[...]) * estimate_scale

    final = [
        send(
            terms.at[pl.ds(peer * out_rows, out_rows)], term_recv.at[i],
            out_send.at[i], out_recv.at[i], {"ap": peer},
        )
        for i, peer in enumerate(peers)
    ]
    result = terms[pl.ds(me * out_rows, out_rows), :]
    for i, copy in reversed(list(enumerate(final))):
        copy.wait_recv()
        result = result + term_recv[i]
    out_ref[...] = result
    for copy in exchange + final:
        copy.wait_send()
    pl.when(has_right)(upward.wait_send)
    pl.when(has_left)(downward.wait_send)


def fused(pilot_received, received, large_scale, pilot_index, serving, user_group):
    n = lax.axis_size("ap")
    sc_count = lax.axis_size("sc")
    _, tau_count, antennas, aps_dev = pilot_received.shape
    symbols = received.shape[3]
    users = pilot_index.shape[0]
    slots = n // 4 * GROUP_SLOTS
    pilot_rows = tau_count * antennas
    out_rows = slots // n
    aps_total = aps_dev * n
    gram_scale = 1.0 / (antennas * aps_total)
    estimate_scale = 1.0 / math.sqrt(antennas * aps_total * serving.shape[1] / users)
    vmem = pl.BlockSpec(memory_space=pltpu.VMEM)
    peers = pltpu.SemaphoreType.DMA((n - 1,))
    two = pltpu.SemaphoreType.DMA((2,))
    out = pl.pallas_call(
        functools.partial(
            fused_kernel, n, sc_count, users, tau_count, antennas, gram_scale, estimate_scale
        ),
        out_shape=pltpu.VMEM((out_rows, symbols), F32),
        in_specs=[pl.BlockSpec(memory_space=pl.ANY)] * 6,
        out_specs=vmem,
        scratch_shapes=[
            pltpu.VMEM((3 * pilot_rows, aps_dev), BF16),
            pltpu.VMEM((antennas * aps_dev, symbols), BF16),
            pltpu.VMEM((users, aps_dev), BF16),
            pltpu.VMEM((1, users), jnp.int32),
            pltpu.VMEM((serving.shape[1], aps_dev), jnp.int32),
            pltpu.VMEM((1, users), jnp.int32),
            pltpu.VMEM((GROUP_SLOTS // 2 + 8, LANES), F32),
            pltpu.VMEM((n - 1, GROUP_SLOTS // 2 + 8, LANES), F32),
            pltpu.VMEM((slots, symbols), F32),
            pltpu.VMEM((n - 1, out_rows, symbols), F32),
            pltpu.SemaphoreType.DMA((6,)),
            two, two, peers, peers, peers, peers, pltpu.SemaphoreType.REGULAR,
        ],
        compiler_params=pltpu.CompilerParams(collective_id=0, has_side_effects=True),
    )(
        pilot_received.reshape(pilot_rows, aps_dev),
        received.reshape(antennas * aps_dev, symbols),
        large_scale,
        pilot_index.reshape(1, users),
        serving.T,
        user_group.reshape(1, users),
    )
    return out.reshape(out_rows, 1, symbols)


def solution(mesh):
    in_specs = (
        P("sc", None, None, "ap"),
        P("sc", None, "ap", None),
        P(None, "ap"),
        P(),
        P("ap", None),
        P(),
    )
    out_specs = P("ap", "sc", None)
    per_device = fused if mesh.shape["ap"] // 4 * GROUP_SLOTS == LANES else on_device
    return jax.shard_map(
        per_device, mesh=mesh, in_specs=in_specs, out_specs=out_specs, check_vma=False
    )
```

```python
import functools
import math

import jax
import jax.numpy as jnp
from jax import lax
from jax.experimental import pallas as pl
from jax.experimental.pallas import tpu as pltpu
from jax.sharding import PartitionSpec as P

GROUP_SLOTS = 64


NOISE_LEVEL = 0.05


def extended_2(block, sides, width):
    for axis, dim in sides:
        count = lax.axis_size(axis)
        forward = [(i, i + 1) for i in range(count - 1)]
        backward = [(target, source) for source, target in forward]
        low = lax.ppermute(
            lax.slice_in_dim(block, block.shape[dim] - width, None, axis=dim), axis, forward
        )
        high = lax.ppermute(lax.slice_in_dim(block, 0, width, axis=dim), axis, backward)
        block = jnp.concatenate([low, block, high], axis=dim)
    return block


def slot_tables(pilot_index, user_group, group_count):
    labels = jnp.arange(group_count, dtype=jnp.int32)
    group_hot = (user_group[:, None] == labels[None, :]).astype(jnp.int32)
    users = jnp.arange(user_group.shape[0], dtype=jnp.int32)
    up_to = (users[:, None] >= users[None, :]).astype(jnp.bfloat16)
    counts = jnp.dot(up_to, group_hot.astype(jnp.bfloat16), preferred_element_type=jnp.float32)
    ranks_in = jnp.sum(counts.astype(jnp.int32) * group_hot, axis=1) - 1
    slot_ids = user_group * GROUP_SLOTS + ranks_in
    members = (
        jnp.zeros((group_count * GROUP_SLOTS,), jnp.int32)
        .at[slot_ids]
        .set(jnp.arange(user_group.shape[0], dtype=jnp.int32))
    )
    occupied = jnp.zeros((group_count * GROUP_SLOTS,), jnp.float32).at[slot_ids].set(1.0)
    slot_pilot = pilot_index[members]
    return (members, occupied, slot_pilot)


def inverse_columns(factor, columns):
    first = lax.linalg.triangular_solve(factor, columns, left_side=True, lower=True)
    return lax.linalg.triangular_solve(factor, first, left_side=True, lower=True, transpose_a=True)


def on_device(pilot_received, received, large_scale, pilot_index, serving, user_group):
    ap_count = lax.axis_size("ap")
    sc_count = lax.axis_size("sc")
    ap_index = lax.axis_index("ap")
    sc_index = lax.axis_index("sc")
    blocks_dev, tau_count, antennas, aps_dev = pilot_received.shape
    symbols = received.shape[3]
    users = pilot_index.shape[0]
    serve_count = serving.shape[1]
    groups = ap_count // 4
    quarter = GROUP_SLOTS // 4
    aps_total = aps_dev * ap_count
    members, occupied, slot_pilot = slot_tables(pilot_index, user_group, groups)
    extended = extended_2(pilot_received, (("sc", 0),), 1)
    block_ids = sc_index * blocks_dev + jnp.arange(blocks_dev, dtype=jnp.int32)
    first_block = (block_ids == 0)[:, None, None, None]
    final_block = (block_ids == blocks_dev * sc_count - 1)[:, None, None, None]
    middle = extended[1:-1].astype(jnp.float32)
    before = jnp.where(first_block, middle, extended[:-2].astype(jnp.float32))
    after = jnp.where(final_block, middle, extended[2:].astype(jnp.float32))
    smooth = 0.25 * before + 0.5 * middle + 0.25 * after
    pilot_hot = (pilot_index[None, :] == jnp.arange(tau_count, dtype=jnp.int32)[:, None]).astype(
        jnp.bfloat16
    )
    contamination = 1.0 + tau_count / users * jnp.dot(
        pilot_hot, large_scale, preferred_element_type=jnp.float32
    )
    serve_mask = (
        jnp.zeros((users, aps_dev), jnp.bfloat16)
        .at[serving, jnp.arange(aps_dev, dtype=jnp.int32)[:, None]]
        .set(1.0)
    )
    batch_groups = min(8, groups)
    batches = groups // batch_groups
    batch_rows = batch_groups * GROUP_SLOTS
    member_blocks = members.reshape(batches, batch_rows)
    occupied_blocks = occupied.reshape(batches, batch_rows)
    pilot_blocks = slot_pilot.reshape(batches, batch_rows)
    gramian_scale = 1.0 / (antennas * aps_total)

    def gram_batch(inputs):
        member_rows, occupied_rows, pilot_rows = inputs
        coeff = (
            occupied_rows[:, None]
            * large_scale[member_rows].astype(jnp.float32)
            * lax.rsqrt(contamination[pilot_rows])
        )
        row_hot = (pilot_rows[:, None] == jnp.arange(tau_count, dtype=jnp.int32)).astype(jnp.float32)
        picked = jnp.einsum("st,btnl->bsnl", row_hot, smooth, precision=lax.Precision.HIGHEST)
        channel_gain = (picked * coeff[None, :, None, :]).astype(jnp.bfloat16)
        channel_gain = channel_gain.reshape(
            blocks_dev, batch_groups, GROUP_SLOTS, antennas * aps_dev
        )
        gram = (
            jnp.einsum(
                "bogx,bohx->ogbh", channel_gain, channel_gain, preferred_element_type=jnp.float32
            )
            * gramian_scale
        )
        return (gram, channel_gain)

    partial_gram, channel_store = lax.map(
        gram_batch, (member_blocks, occupied_blocks, pilot_blocks)
    )
    partial_gram = partial_gram.reshape(groups * GROUP_SLOTS, blocks_dev, GROUP_SLOTS)
    summed = lax.psum(partial_gram, "ap")
    owned = lax.dynamic_slice_in_dim(summed, ap_index // 4 * GROUP_SLOTS, GROUP_SLOTS, 0)
    identity = jnp.eye(GROUP_SLOTS, dtype=jnp.float32)
    system = jnp.transpose(owned, (1, 0, 2)) + NOISE_LEVEL * identity
    factor = jnp.linalg.cholesky(system)
    columns = lax.dynamic_slice_in_dim(identity, ap_index % 4 * quarter, quarter, 1)
    solved = inverse_columns(factor, jnp.broadcast_to(columns, (blocks_dev, GROUP_SLOTS, quarter)))
    weight_rows = jnp.transpose(solved, (2, 0, 1)).astype(jnp.bfloat16)
    all_weights = lax.all_gather(weight_rows, "ap", axis=0, tiled=True)
    weight_blocks = all_weights.reshape(batches, batch_groups, GROUP_SLOTS, blocks_dev, GROUP_SLOTS)
    data_signal = received.reshape(blocks_dev, antennas * aps_dev, symbols)
    estimator_scale = 1.0 / math.sqrt(antennas * aps_total * serve_count / users)

    def estimate_batch(inputs):
        member_rows, occupied_rows, channel_gain, weights = inputs
        combiner_weight = jnp.einsum(
            "okbj,bojx->bokx", weights, channel_gain, preferred_element_type=jnp.float32
        ).astype(jnp.bfloat16)
        row_mask_values = serve_mask[member_rows] * occupied_rows[:, None].astype(jnp.bfloat16)
        masked_values = (
            combiner_weight.reshape(blocks_dev, batch_rows, antennas, aps_dev)
            * row_mask_values[None, :, None, :]
        )
        flattened_masked = masked_values.reshape(blocks_dev, batch_rows, antennas * aps_dev)
        return (
            jnp.einsum(
                "bsx,bxt->sbt", flattened_masked, data_signal, preferred_element_type=jnp.float32
            )
            * estimator_scale
        )

    terms = lax.map(estimate_batch, (member_blocks, occupied_blocks, channel_store, weight_blocks))
    terms = terms.reshape(groups * GROUP_SLOTS, blocks_dev, symbols)
    return lax.psum_scatter(terms, "ap", scatter_dimension=0, tiled=True)


LANES = 128
BF16 = jnp.bfloat16
F32 = jnp.float32
NT = (((1,), (1,)), ((), ()))


def iota(shape, dim):
    return lax.broadcasted_iota(jnp.int32, shape, dim)


def mm(a, b, dims=(((1,), (0,)), ((), ()))):
    return lax.dot_general(a, b, dims, preferred_element_type=F32)


def total_of(terms):
    while len(terms) > 1:
        pairs = [a + b for a, b in zip(terms[::2], terms[1::2])]
        terms = pairs + terms[len(terms) // 2 * 2 :]
    return terms[0]


def invert_pairs(mat):
    tile = 8
    inner = iota((tile, LANES), 1) % GROUP_SLOTS
    base = iota((tile, LANES), 1) - inner
    sub = iota((tile, LANES), 0)
    parts = [mat[i : i + tile] for i in range(0, GROUP_SLOTS, tile)]

    def line_of(part, line):
        return jnp.broadcast_to(part[line : line + 1], (tile, LANES))

    for home in range(len(parts)):
        start = home * tile
        columns = [
            [jnp.take_along_axis(part, base + start + k, axis=1) for part in parts] for k in range(tile)
        ]
        ahead = [column[home] for column in columns]
        rows = parts[home]
        for j in range(0, tile, 2):
            first, second = ahead[j], ahead[j + 1]
            p00, p01, p11 = line_of(first, j), line_of(second, j), line_of(second, j + 1)
            scale = 1.0 / (p00 * p11 - p01 * p01)
            lines = sub // 2 == j // 2
            first = jnp.where(sub == j, -1.0, jnp.where(sub == j + 1, 0.0, first))
            second = jnp.where(sub == j + 1, -1.0, jnp.where(sub == j, 0.0, second))

            def reduced(kept, upper, lower):
                above, below = p11 * upper - p01 * lower, p00 * lower - p01 * upper
                return kept - (first * above + second * below) * scale

            for k in range(j + 2, tile):
                kept = jnp.where(lines, 0.0, ahead[k])
                ahead[k] = reduced(kept, line_of(ahead[k], j), line_of(ahead[k], j + 1))
            here, there = inner == start + j, inner == start + j + 1
            kept = jnp.where(lines | here | there, 0.0, rows)
            upper = jnp.where(here, 1.0, jnp.where(there, 0.0, line_of(rows, j)))
            lower = jnp.where(there, 1.0, jnp.where(here, 0.0, line_of(rows, j + 1)))
            rows = reduced(kept, upper, lower)
        lines = [line_of(rows, k) for k in range(tile)]
        within = inner // tile == home
        parts = [
            rows
            if i == home
            else jnp.where(within, 0.0, part) - total_of([columns[k][i] * lines[k] for k in range(tile)])
            for i, part in enumerate(parts)
        ]
    return jnp.concatenate(parts, axis=0)


def fused_kernel(
    n, sc_count, users, tau_count, antennas, gram_scale, estimate_scale,
    pilot_ref, data_ref, large_ref, pilot_index_ref, serving_ref, group_ref,
    out_ref,
    pilots, data, large_in, pilot_index, serving_in, group_in,
    grams, terms, term_recv,
    load, halo_send, halo_recv, gram_send, gram_arrive, out_send, out_recv, ready, side,
):
    me = lax.axis_index("ap")
    sc = lax.axis_index("sc")
    right, left = sc + 1, sc - 1
    pilot_rows = tau_count * antennas
    small = users - GROUP_SLOTS
    out_rows = n // 4 * GROUP_SLOTS // n

    loads = []
    for source, target in (
        (group_ref, group_in), (pilot_index_ref, pilot_index), (large_ref, large_in),
        (pilot_ref, pilots.at[pl.ds(pilot_rows, pilot_rows)]), (serving_ref, serving_in), (data_ref, data),
    ):
        loads.append(pltpu.make_async_copy(source, target, load.at[len(loads)]))
        loads[-1].start()

    def signal(semaphore, **where):
        pl.semaphore_signal(semaphore, inc=1, device_id=where, device_id_type=pl.DeviceIdType.MESH)

    barrier = pltpu.get_barrier_semaphore()
    even = sc % 2 == 0
    has_left, has_right = sc > 0, sc < sc_count - 1
    pl.when(has_right)(functools.partial(signal, barrier, sc=right))
    pl.when(has_left & jnp.logical_not(even))(functools.partial(signal, barrier, sc=left))

    @pl.loop(me + 1, n)
    def _(peer):
        signal(barrier, ap=peer)


    def make(src, dst, send_sem, recv_sem, where):
        return pltpu.make_async_remote_copy(
            src_ref=src, dst_ref=dst, send_sem=send_sem, recv_sem=recv_sem,
            device_id=where, device_id_type=pl.DeviceIdType.MESH,
        )

    middle = pilots.at[pl.ds(pilot_rows, pilot_rows)]
    first, last = (pilots.at[pl.ds(i * pilot_rows, pilot_rows)] for i in (0, 2))
    upward = make(pilot_ref, first, halo_send.at[0], halo_recv.at[0], {"sc": right})
    upward_later = make(middle, first, halo_send.at[0], halo_recv.at[0], {"sc": right})
    downward = make(pilot_ref, last, halo_send.at[1], halo_recv.at[1], {"sc": left})
    entered = has_left.astype(jnp.int32) + (even & has_right).astype(jnp.int32)
    pl.semaphore_wait(barrier, me + entered)
    pl.when(has_left & even)(functools.partial(signal, side, sc=left))
    pl.when(has_left)(downward.start)
    pl.when(has_right & even)(upward.start)

    @pl.loop(0, me)
    def _(peer):
        signal(ready.at[me], ap=peer)

    blank = jnp.zeros((pilot_rows, pilots.shape[1]), BF16)

    @pl.when(jnp.logical_not(has_left))
    def _():
        pilots[pl.ds(0, pilot_rows), :] = blank

    @pl.when(jnp.logical_not(has_right))
    def _():
        pilots[pl.ds(2 * pilot_rows, pilot_rows), :] = blank

    for copy in loads[:3]:
        copy.wait()
    group = group_in[...]
    wide = (users, 2 * LANES)
    earlier = jnp.where((iota(wide, 0) < iota(wide, 1)) | (iota(wide, 1) >= LANES), 1.0, 0.0)
    counts = mm(jnp.broadcast_to(group, (8, users)).astype(F32).astype(BF16), earlier.astype(BF16))
    later_group = counts[:1, :users].astype(jnp.int32)
    second_large = counts[:1, LANES:] > GROUP_SLOTS - 0.5
    rank = jnp.where(group == 1, later_group, iota(group.shape, 1) - later_group)
    is_large = (group == 1) == second_large[:, :users]
    slot_row = jnp.where(is_large, rank, rank + GROUP_SLOTS)
    hot = jnp.where(iota((users, users), 0) == slot_row, 1.0, 0.0).astype(BF16)
    tall = (LANES, users)
    facts = jnp.concatenate(
        [jnp.broadcast_to(pilot_index[...], tall).astype(F32), iota(tall, 1).astype(F32)], axis=0
    )
    facts = mm(hot, facts.astype(BF16), NT)
    slot_pilot, member = facts[:, :LANES].astype(jnp.int32), facts[:, LANES:].astype(jnp.int32)
    same_pilot = jnp.where(slot_pilot[:, :users] == pilot_index[...], 1.0, 0.0).astype(BF16)
    large = large_in[...]
    contamination = 1.0 + tau_count / users * mm(same_pilot, large)
    coeff = mm(hot, large) * lax.rsqrt(contamination)

    low = jnp.where(sc == 0, 0.0, 0.25)
    high = jnp.where(sc == sc_count - 1, 0.0, 0.25)
    lane = iota((users, LANES), 1)
    meets = slot_pilot == lane % pilot_rows // antennas
    early = jnp.where(meets, jnp.where(lane < pilot_rows, low, 1.0 - low - high), 0.0)
    late = jnp.where(meets, high, 0.0)
    spread = jnp.concatenate(
        [
            jnp.concatenate(
                [
                    jnp.where(lane % antennas == a, early, 0.0).astype(BF16),
                    jnp.where(lane % antennas == a, late, 0.0).astype(BF16)[:, :pilot_rows],
                ],
                axis=1,
            )
            for a in range(antennas)
        ],
        axis=0,
    )

    loads[3].wait()

    @pl.when(has_right & jnp.logical_not(even))
    def _():
        pl.semaphore_wait(side, 1)
        upward_later.start()

    pl.when(has_left)(upward.wait_recv)
    pl.when(has_right)(downward.wait_recv)
    smooth = mm(spread, pilots[...])
    channel = jnp.concatenate(
        [(smooth[a * users : (a + 1) * users] * coeff).astype(BF16) for a in range(antennas)], axis=1
    )
    channel = jnp.concatenate([channel, jnp.zeros((LANES - users, channel.shape[1]), BF16)], axis=0)
    gram = mm(channel[:users], channel, NT) * gram_scale

    def turn(part, amount):
        return pltpu.roll(part, amount % LANES, 1)

    lane, row = iota((small, LANES), 1), iota((small, LANES), 0)
    top, bottom, other = (gram[i * small : (i + 1) * small] for i in range(3))
    packed = jnp.where(lane < row, turn(bottom, -small), jnp.where(lane < GROUP_SLOTS, top, other))
    last = packed[small - 8 :]
    eight = iota((8, LANES), 1)
    for i in range(3):
        grams[me, pl.ds(8 * i, 8), :] = jnp.where(
            eight < users, packed[8 * i : 8 * i + 8], turn(last, users - small * i)
        )
    diagonal = [
        jnp.where(lane == row + i * small, part, 0.0) for i, part in enumerate((top, bottom, other))
    ]
    gram_rows = small - 7
    grams[me, pl.ds(gram_rows - 1, 1), :] = jnp.sum(total_of(diagonal), axis=0, keepdims=True)
    own = grams.at[me, pl.ds(0, gram_rows)]

    @pl.loop(0, me)
    def _(peer):
        make(own, own, gram_send, gram_arrive, {"ap": peer}).start()

    @pl.loop(me + 1, n)
    def _(peer):
        pl.semaphore_wait(ready.at[peer], 1)
        make(own, own, gram_send, gram_arrive, {"ap": peer}).start()

    for copy in loads[4:]:
        copy.wait()
    serving = serving_in[...]
    mask = jnp.zeros((users, serving.shape[1]), F32)
    for j in range(serving.shape[0]):
        mask = jnp.where(member == serving[j : j + 1, :], 1.0, mask)
    mask = mask.astype(BF16)

    every = grams.at[pl.ds(0, n - 1), pl.ds(0, gram_rows)]
    pltpu.make_async_copy(every, every, gram_arrive).wait()
    total = total_of([grams[i, pl.ds(0, gram_rows), :] for i in range(n)])
    parts = [total[8 * i : 8 * i + 8] for i in range(3)]
    last = jnp.where(eight < 2 * small, turn(parts[1], small - users), turn(parts[2], 2 * small - users))
    last = jnp.where(eight < small, turn(parts[0], -users), last)
    packed = jnp.concatenate(parts + [last], axis=0)
    shifted, shifted_twice = turn(packed, small), turn(packed, 2 * small)
    mirrored = jnp.transpose(jnp.concatenate([packed, shifted, shifted_twice, shifted_twice], axis=0))
    within = lane % GROUP_SLOTS >= row
    upper = jnp.where(within, packed, mirrored[:small])
    upper = jnp.where(lane < users, upper, 0.0)
    lower = jnp.where((lane >= small) & (lane - small < row), shifted, mirrored[small : 2 * small])
    lower = jnp.where(lane < GROUP_SLOTS, lower, 0.0)
    system = jnp.concatenate([upper, lower], axis=0)
    lane, row = iota(system.shape, 1), iota(system.shape, 0)
    system = jnp.where(lane % GROUP_SLOTS == row, total[gram_rows - 1 : gram_rows] + NOISE_LEVEL, system)
    inverse = invert_pairs(system)
    weights = jnp.concatenate(
        [
            jnp.where(lane < GROUP_SLOTS, inverse, 0.0),
            jnp.where((lane >= GROUP_SLOTS) & (lane < users), inverse, 0.0)[:small],
        ],
        axis=0,
    ).astype(BF16)
    combine = mm(weights, channel).astype(BF16)
    masked = combine * jnp.concatenate([mask] * antennas, axis=1)
    found = mm(masked, data[...]) * estimate_scale
    large_group = found[:GROUP_SLOTS]
    small_group = jnp.concatenate([found[GROUP_SLOTS:], jnp.zeros((GROUP_SLOTS - small, LANES), F32)], axis=0)
    terms[pl.ds(0, GROUP_SLOTS), :] = jnp.where(second_large, small_group, large_group)
    terms[pl.ds(GROUP_SLOTS, GROUP_SLOTS), :] = jnp.where(second_large, large_group, small_group)

    def give(peer):
        make(
            terms.at[pl.ds(peer * out_rows, out_rows)], term_recv.at[me], out_send, out_recv, {"ap": peer}
        ).start()

    pl.loop(0, me)(give)
    pl.loop(me + 1, n)(give)
    term_recv[me] = terms[pl.ds(me * out_rows, out_rows), :]
    shares = term_recv.at[pl.ds(0, n - 1)]
    pltpu.make_async_copy(shares, shares, out_recv).wait()
    out_ref[...] = total_of([term_recv[i] for i in range(n)])
    pltpu.make_async_copy(every, every, gram_send).wait()
    pltpu.make_async_copy(shares, shares, out_send).wait()
    pl.when(has_right)(upward.wait_send)
    pl.when(has_left)(downward.wait_send)


def fused(pilot_received, received, large_scale, pilot_index, serving, user_group):
    n = lax.axis_size("ap")
    sc_count = lax.axis_size("sc")
    _, tau_count, antennas, aps_dev = pilot_received.shape
    symbols = received.shape[3]
    users = pilot_index.shape[0]
    slots = n // 4 * GROUP_SLOTS
    pilot_rows = tau_count * antennas
    out_rows = slots // n
    aps_total = aps_dev * n
    gram_scale = 1.0 / (antennas * aps_total)
    estimate_scale = 1.0 / math.sqrt(antennas * aps_total * serving.shape[1] / users)
    vmem = pl.BlockSpec(memory_space=pltpu.VMEM)
    two = pltpu.SemaphoreType.DMA((2,))
    one = pltpu.SemaphoreType.DMA
    out = pl.pallas_call(
        functools.partial(
            fused_kernel, n, sc_count, users, tau_count, antennas, gram_scale, estimate_scale
        ),
        out_shape=pltpu.VMEM((out_rows, symbols), F32),
        in_specs=[pl.BlockSpec(memory_space=pl.ANY)] * 6,
        out_specs=vmem,
        scratch_shapes=[
            pltpu.VMEM((3 * pilot_rows, aps_dev), BF16),
            pltpu.VMEM((antennas * aps_dev, symbols), BF16),
            pltpu.VMEM((users, aps_dev), BF16),
            pltpu.VMEM((1, users), jnp.int32),
            pltpu.VMEM((serving.shape[1], aps_dev), jnp.int32),
            pltpu.VMEM((1, users), jnp.int32),
            pltpu.VMEM((n, GROUP_SLOTS // 2, LANES), F32),
            pltpu.VMEM((slots, symbols), F32),
            pltpu.VMEM((n, out_rows, symbols), F32),
            pltpu.SemaphoreType.DMA((6,)),
            two, two, one, one, one, one, pltpu.SemaphoreType.REGULAR((n,)), pltpu.SemaphoreType.REGULAR,
        ],
        compiler_params=pltpu.CompilerParams(collective_id=0, has_side_effects=True),
    )(
        pilot_received.reshape(pilot_rows, aps_dev),
        received.reshape(antennas * aps_dev, symbols),
        large_scale,
        pilot_index.reshape(1, users),
        serving.T,
        user_group.reshape(1, users),
    )
    return out.reshape(out_rows, 1, symbols)


def solution(mesh):
    in_specs = (
        P("sc", None, None, "ap"),
        P("sc", None, "ap", None),
        P(None, "ap"),
        P(),
        P("ap", None),
        P(),
    )
    out_specs = P("ap", "sc", None)

    def per_device(*arguments):
        slots = mesh.shape["ap"] // 4 * GROUP_SLOTS
        users = arguments[3].shape[0]
        filled = slots == LANES and 4 * users == 3 * slots
        return (fused if filled else on_device)(*arguments)

    return jax.shard_map(
        per_device, mesh=mesh, in_specs=in_specs, out_specs=out_specs, check_vma=False
    )
```

```python
import functools
import math

import jax
import jax.numpy as jnp
from jax import lax
from jax.experimental import pallas as pl
from jax.experimental.pallas import tpu as pltpu
from jax.sharding import PartitionSpec as P

GROUP_SLOTS = 64


NOISE_LEVEL = 0.05


def extended_2(block, sides, width):
    for axis, dim in sides:
        count = lax.axis_size(axis)
        forward = [(i, i + 1) for i in range(count - 1)]
        backward = [(target, source) for source, target in forward]
        low = lax.ppermute(
            lax.slice_in_dim(block, block.shape[dim] - width, None, axis=dim), axis, forward
        )
        high = lax.ppermute(lax.slice_in_dim(block, 0, width, axis=dim), axis, backward)
        block = jnp.concatenate([low, block, high], axis=dim)
    return block


def slot_tables(pilot_index, user_group, group_count):
    labels = jnp.arange(group_count, dtype=jnp.int32)
    group_hot = (user_group[:, None] == labels[None, :]).astype(jnp.int32)
    users = jnp.arange(user_group.shape[0], dtype=jnp.int32)
    up_to = (users[:, None] >= users[None, :]).astype(jnp.bfloat16)
    counts = jnp.dot(up_to, group_hot.astype(jnp.bfloat16), preferred_element_type=jnp.float32)
    ranks_in = jnp.sum(counts.astype(jnp.int32) * group_hot, axis=1) - 1
    slot_ids = user_group * GROUP_SLOTS + ranks_in
    members = (
        jnp.zeros((group_count * GROUP_SLOTS,), jnp.int32)
        .at[slot_ids]
        .set(jnp.arange(user_group.shape[0], dtype=jnp.int32))
    )
    occupied = jnp.zeros((group_count * GROUP_SLOTS,), jnp.float32).at[slot_ids].set(1.0)
    slot_pilot = pilot_index[members]
    return (members, occupied, slot_pilot)


def inverse_columns(factor, columns):
    first = lax.linalg.triangular_solve(factor, columns, left_side=True, lower=True)
    return lax.linalg.triangular_solve(factor, first, left_side=True, lower=True, transpose_a=True)


def on_device(pilot_received, received, large_scale, pilot_index, serving, user_group):
    ap_count = lax.axis_size("ap")
    sc_count = lax.axis_size("sc")
    ap_index = lax.axis_index("ap")
    sc_index = lax.axis_index("sc")
    blocks_dev, tau_count, antennas, aps_dev = pilot_received.shape
    symbols = received.shape[3]
    users = pilot_index.shape[0]
    serve_count = serving.shape[1]
    groups = ap_count // 4
    quarter = GROUP_SLOTS // 4
    aps_total = aps_dev * ap_count
    members, occupied, slot_pilot = slot_tables(pilot_index, user_group, groups)
    extended = extended_2(pilot_received, (("sc", 0),), 1)
    block_ids = sc_index * blocks_dev + jnp.arange(blocks_dev, dtype=jnp.int32)
    first_block = (block_ids == 0)[:, None, None, None]
    final_block = (block_ids == blocks_dev * sc_count - 1)[:, None, None, None]
    middle = extended[1:-1].astype(jnp.float32)
    before = jnp.where(first_block, middle, extended[:-2].astype(jnp.float32))
    after = jnp.where(final_block, middle, extended[2:].astype(jnp.float32))
    smooth = 0.25 * before + 0.5 * middle + 0.25 * after
    pilot_hot = (pilot_index[None, :] == jnp.arange(tau_count, dtype=jnp.int32)[:, None]).astype(
        jnp.bfloat16
    )
    contamination = 1.0 + tau_count / users * jnp.dot(
        pilot_hot, large_scale, preferred_element_type=jnp.float32
    )
    serve_mask = (
        jnp.zeros((users, aps_dev), jnp.bfloat16)
        .at[serving, jnp.arange(aps_dev, dtype=jnp.int32)[:, None]]
        .set(1.0)
    )
    batch_groups = min(8, groups)
    batches = groups // batch_groups
    batch_rows = batch_groups * GROUP_SLOTS
    member_blocks = members.reshape(batches, batch_rows)
    occupied_blocks = occupied.reshape(batches, batch_rows)
    pilot_blocks = slot_pilot.reshape(batches, batch_rows)
    gramian_scale = 1.0 / (antennas * aps_total)

    def gram_batch(inputs):
        member_rows, occupied_rows, pilot_rows = inputs
        coeff = (
            occupied_rows[:, None]
            * large_scale[member_rows].astype(jnp.float32)
            * lax.rsqrt(contamination[pilot_rows])
        )
        row_hot = (pilot_rows[:, None] == jnp.arange(tau_count, dtype=jnp.int32)).astype(jnp.float32)
        picked = jnp.einsum("st,btnl->bsnl", row_hot, smooth, precision=lax.Precision.HIGHEST)
        channel_gain = (picked * coeff[None, :, None, :]).astype(jnp.bfloat16)
        channel_gain = channel_gain.reshape(
            blocks_dev, batch_groups, GROUP_SLOTS, antennas * aps_dev
        )
        gram = (
            jnp.einsum(
                "bogx,bohx->ogbh", channel_gain, channel_gain, preferred_element_type=jnp.float32
            )
            * gramian_scale
        )
        return (gram, channel_gain)

    partial_gram, channel_store = lax.map(
        gram_batch, (member_blocks, occupied_blocks, pilot_blocks)
    )
    partial_gram = partial_gram.reshape(groups * GROUP_SLOTS, blocks_dev, GROUP_SLOTS)
    summed = lax.psum(partial_gram, "ap")
    owned = lax.dynamic_slice_in_dim(summed, ap_index // 4 * GROUP_SLOTS, GROUP_SLOTS, 0)
    identity = jnp.eye(GROUP_SLOTS, dtype=jnp.float32)
    system = jnp.transpose(owned, (1, 0, 2)) + NOISE_LEVEL * identity
    factor = jnp.linalg.cholesky(system)
    columns = lax.dynamic_slice_in_dim(identity, ap_index % 4 * quarter, quarter, 1)
    solved = inverse_columns(factor, jnp.broadcast_to(columns, (blocks_dev, GROUP_SLOTS, quarter)))
    weight_rows = jnp.transpose(solved, (2, 0, 1)).astype(jnp.bfloat16)
    all_weights = lax.all_gather(weight_rows, "ap", axis=0, tiled=True)
    weight_blocks = all_weights.reshape(batches, batch_groups, GROUP_SLOTS, blocks_dev, GROUP_SLOTS)
    data_signal = received.reshape(blocks_dev, antennas * aps_dev, symbols)
    estimator_scale = 1.0 / math.sqrt(antennas * aps_total * serve_count / users)

    def estimate_batch(inputs):
        member_rows, occupied_rows, channel_gain, weights = inputs
        combiner_weight = jnp.einsum(
            "okbj,bojx->bokx", weights, channel_gain, preferred_element_type=jnp.float32
        ).astype(jnp.bfloat16)
        row_mask_values = serve_mask[member_rows] * occupied_rows[:, None].astype(jnp.bfloat16)
        masked_values = (
            combiner_weight.reshape(blocks_dev, batch_rows, antennas, aps_dev)
            * row_mask_values[None, :, None, :]
        )
        flattened_masked = masked_values.reshape(blocks_dev, batch_rows, antennas * aps_dev)
        return (
            jnp.einsum(
                "bsx,bxt->sbt", flattened_masked, data_signal, preferred_element_type=jnp.float32
            )
            * estimator_scale
        )

    terms = lax.map(estimate_batch, (member_blocks, occupied_blocks, channel_store, weight_blocks))
    terms = terms.reshape(groups * GROUP_SLOTS, blocks_dev, symbols)
    return lax.psum_scatter(terms, "ap", scatter_dimension=0, tiled=True)


LANES = 128
BF16 = jnp.bfloat16
F32 = jnp.float32
NT = (((1,), (1,)), ((), ()))


def iota(shape, dim):
    return lax.broadcasted_iota(jnp.int32, shape, dim)


def mm(a, b, dims=(((1,), (0,)), ((), ()))):
    return lax.dot_general(a, b, dims, preferred_element_type=F32)


def total_of(terms):
    while len(terms) > 1:
        pairs = [a + b for a, b in zip(terms[::2], terms[1::2])]
        terms = pairs + terms[len(terms) // 2 * 2 :]
    return terms[0]


def invert_pairs(mat):
    tile = 8
    inner = iota((tile, LANES), 1) % GROUP_SLOTS
    base = iota((tile, LANES), 1) - inner
    sub = iota((tile, LANES), 0)
    parts = [mat[i : i + tile] for i in range(0, GROUP_SLOTS, tile)]

    def line_of(part, line):
        return jnp.broadcast_to(part[line : line + 1], (tile, LANES))

    for home in range(len(parts)):
        start = home * tile
        rows = parts[home]
        spread = [line_of(rows, k) for k in range(tile)]
        ahead = [jnp.take_along_axis(line, base + start + sub, axis=1) for line in spread]
        columns = [
            [jnp.take_along_axis(line, base + tile * i + sub, axis=1) for line in spread]
            for i in range(len(parts))
        ]
        for j in range(0, tile, 2):
            first, second = ahead[j], ahead[j + 1]
            p00, p01, p11 = line_of(first, j), line_of(second, j), line_of(second, j + 1)
            scale = 1.0 / (p00 * p11 - p01 * p01)
            lines = sub // 2 == j // 2
            first = jnp.where(sub == j, -1.0, jnp.where(sub == j + 1, 0.0, first))
            second = jnp.where(sub == j + 1, -1.0, jnp.where(sub == j, 0.0, second))

            def reduced(kept, upper, lower):
                above, below = p11 * upper - p01 * lower, p00 * lower - p01 * upper
                return kept - (first * above + second * below) * scale

            for k in range(j + 2, tile):
                kept = jnp.where(lines, 0.0, ahead[k])
                ahead[k] = reduced(kept, line_of(ahead[k], j), line_of(ahead[k], j + 1))
            here, there = inner == start + j, inner == start + j + 1
            kept = jnp.where(lines | here | there, 0.0, rows)
            upper = jnp.where(here, 1.0, jnp.where(there, 0.0, line_of(rows, j)))
            lower = jnp.where(there, 1.0, jnp.where(here, 0.0, line_of(rows, j + 1)))
            rows = reduced(kept, upper, lower)
        lines = [line_of(rows, k) for k in range(tile)]
        within = inner // tile == home
        parts = [
            rows
            if i == home
            else (jnp.where(within, 0.0, part) - change if i > home else jnp.where(within, 0.0, part) + change)
            for i, (part, change) in enumerate(
                zip(parts, [total_of([a * b for a, b in zip(column, lines)]) for column in columns])
            )
        ]
    return jnp.concatenate(parts, axis=0)


def fused_kernel(
    n, sc_count, users, tau_count, antennas, gram_scale, estimate_scale,
    pilot_ref, data_ref, large_ref, pilot_index_ref, serving_ref, group_ref,
    out_ref,
    pilots, data, large_in, pilot_index, serving_in, group_in,
    grams, terms, term_recv,
    load, halo_send, halo_recv, gram_send, gram_arrive, out_send, out_recv, ready, side,
):
    me = lax.axis_index("ap")
    sc = lax.axis_index("sc")
    right, left = sc + 1, sc - 1
    pilot_rows = tau_count * antennas
    small = users - GROUP_SLOTS
    out_rows = n // 4 * GROUP_SLOTS // n

    loads = []
    for source, target in (
        (group_ref, group_in), (pilot_index_ref, pilot_index), (large_ref, large_in),
        (pilot_ref, pilots.at[pl.ds(pilot_rows, pilot_rows)]), (serving_ref, serving_in), (data_ref, data),
    ):
        loads.append(pltpu.make_async_copy(source, target, load.at[len(loads)]))
        loads[-1].start()

    def signal(semaphore, **where):
        pl.semaphore_signal(semaphore, inc=1, device_id=where, device_id_type=pl.DeviceIdType.MESH)

    barrier = pltpu.get_barrier_semaphore()
    even = sc % 2 == 0
    has_left, has_right = sc > 0, sc < sc_count - 1
    pl.when(has_right)(functools.partial(signal, barrier, sc=right))
    pl.when(has_left & jnp.logical_not(even))(functools.partial(signal, barrier, sc=left))

    anchors = jnp.where(has_left, 0, n)
    anchor = me < anchors

    @pl.loop(me + 1, n)
    def _(peer):
        signal(barrier, ap=peer)

    @pl.loop(0, jnp.minimum(anchors, me))
    def _(peer):
        signal(barrier, ap=peer)


    def make(src, dst, send_sem, recv_sem, where):
        return pltpu.make_async_remote_copy(
            src_ref=src, dst_ref=dst, send_sem=send_sem, recv_sem=recv_sem,
            device_id=where, device_id_type=pl.DeviceIdType.MESH,
        )

    middle = pilots.at[pl.ds(pilot_rows, pilot_rows)]
    first, last = (pilots.at[pl.ds(i * pilot_rows, pilot_rows)] for i in (0, 2))
    upward = make(pilot_ref, first, halo_send.at[0], halo_recv.at[0], {"sc": right})
    upward_later = make(middle, first, halo_send.at[0], halo_recv.at[0], {"sc": right})
    downward = make(pilot_ref, last, halo_send.at[1], halo_recv.at[1], {"sc": left})
    entered = has_left.astype(jnp.int32) + (even & has_right).astype(jnp.int32)

    def enter():
        pl.semaphore_wait(barrier, entered + jnp.where(anchor, n - 1, me))
        pl.when(has_left & even)(functools.partial(signal, side, sc=left))
        pl.when(has_left)(downward.start)
        pl.when(has_right & even)(upward.start)

        @pl.loop(anchors, me)
        def _(peer):
            signal(ready.at[me], ap=peer)

    pl.when(jnp.logical_not(anchor))(enter)
    blank = jnp.zeros((pilot_rows, pilots.shape[1]), BF16)

    @pl.when(jnp.logical_not(has_left))
    def _():
        pilots[pl.ds(0, pilot_rows), :] = blank

    @pl.when(jnp.logical_not(has_right))
    def _():
        pilots[pl.ds(2 * pilot_rows, pilot_rows), :] = blank

    for copy in loads[:3]:
        copy.wait()
    group = group_in[...]
    wide = (users, 2 * LANES)
    earlier = jnp.where((iota(wide, 0) < iota(wide, 1)) | (iota(wide, 1) >= LANES), 1.0, 0.0)
    counts = mm(jnp.broadcast_to(group, (8, users)).astype(F32).astype(BF16), earlier.astype(BF16))
    later_group = counts[:1, :users].astype(jnp.int32)
    second_large = counts[:1, LANES:] > GROUP_SLOTS - 0.5
    rank = jnp.where(group == 1, later_group, iota(group.shape, 1) - later_group)
    is_large = (group == 1) == second_large[:, :users]
    slot_row = jnp.where(is_large, rank, rank + GROUP_SLOTS)
    hot = jnp.where(iota((users, users), 0) == slot_row, 1.0, 0.0).astype(BF16)
    tall = (LANES, users)
    facts = jnp.concatenate(
        [jnp.broadcast_to(pilot_index[...], tall).astype(F32), iota(tall, 1).astype(F32)], axis=0
    )
    facts = mm(hot, facts.astype(BF16), NT)
    slot_pilot, member = facts[:, :LANES].astype(jnp.int32), facts[:, LANES:].astype(jnp.int32)
    same_pilot = jnp.where(slot_pilot[:, :users] == pilot_index[...], 1.0, 0.0).astype(BF16)
    large = large_in[...]
    contamination = 1.0 + tau_count / users * mm(same_pilot, large)
    coeff = mm(hot, large) * lax.rsqrt(contamination)

    low = jnp.where(sc == 0, 0.0, 0.25)
    high = jnp.where(sc == sc_count - 1, 0.0, 0.25)
    lane = iota((users, LANES), 1)
    meets = slot_pilot == lane % pilot_rows // antennas
    early = jnp.where(meets, jnp.where(lane < pilot_rows, low, 1.0 - low - high), 0.0)
    late = jnp.where(meets, high, 0.0)
    spread = jnp.concatenate(
        [
            jnp.concatenate(
                [
                    jnp.where(lane % antennas == a, early, 0.0).astype(BF16),
                    jnp.where(lane % antennas == a, late, 0.0).astype(BF16)[:, :pilot_rows],
                ],
                axis=1,
            )
            for a in range(antennas)
        ],
        axis=0,
    )

    loads[3].wait()

    @pl.when(has_right & jnp.logical_not(even))
    def _():
        pl.semaphore_wait(side, 1)
        upward_later.start()

    pl.when(has_left)(upward.wait_recv)
    pl.when(has_right)(downward.wait_recv)
    smooth = mm(spread, pilots[...])
    channel = jnp.concatenate(
        [(smooth[a * users : (a + 1) * users] * coeff).astype(BF16) for a in range(antennas)], axis=1
    )
    channel = jnp.concatenate([channel, jnp.zeros((LANES - users, channel.shape[1]), BF16)], axis=0)
    gram = mm(channel[:users], channel, NT) * gram_scale

    def turn(part, amount):
        return pltpu.roll(part, amount % LANES, 1)

    lane, row = iota((small, LANES), 1), iota((small, LANES), 0)
    top, bottom, other = (gram[i * small : (i + 1) * small] for i in range(3))
    packed = jnp.where(lane < row, turn(bottom, -small), jnp.where(lane < GROUP_SLOTS, top, other))
    last = packed[small - 8 :]
    eight = iota((8, LANES), 1)
    for i in range(3):
        grams[me, pl.ds(8 * i, 8), :] = jnp.where(
            eight < users, packed[8 * i : 8 * i + 8], turn(last, users - small * i)
        )
    diagonal = [
        jnp.where(lane == row + i * small, part, 0.0) for i, part in enumerate((top, bottom, other))
    ]
    gram_rows = small - 7
    grams[me, pl.ds(gram_rows - 1, 1), :] = jnp.sum(total_of(diagonal), axis=0, keepdims=True)
    own = grams.at[me, pl.ds(0, gram_rows)]
    pl.when(anchor)(enter)

    @pl.loop(0, n - 1)
    def _(i):
        down = n - 1 - i
        peer = jnp.where(anchor, jnp.where(down > me, down, down - 1), jnp.where(i < me, i, i + 1))

        @pl.when(jnp.logical_not(anchor) & (peer > me))
        def _():
            pl.semaphore_wait(ready.at[peer], 1)

        make(own, own, gram_send, gram_arrive, {"ap": peer}).start()

    for copy in loads[4:]:
        copy.wait()
    serving = serving_in[...]
    mask = jnp.zeros((users, serving.shape[1]), F32)
    for j in range(serving.shape[0]):
        mask = jnp.where(member == serving[j : j + 1, :], 1.0, mask)
    mask = mask.astype(BF16)

    every = grams.at[pl.ds(0, n - 1), pl.ds(0, gram_rows)]
    pltpu.make_async_copy(every, every, gram_arrive).wait()
    total = total_of([grams[i, pl.ds(0, gram_rows), :] for i in range(n)])
    parts = [total[8 * i : 8 * i + 8] for i in range(3)]
    last = jnp.where(eight < 2 * small, turn(parts[1], small - users), turn(parts[2], 2 * small - users))
    last = jnp.where(eight < small, turn(parts[0], -users), last)
    packed = jnp.concatenate(parts + [last], axis=0)
    shifted, shifted_twice = turn(packed, small), turn(packed, 2 * small)
    mirrored = jnp.transpose(jnp.concatenate([packed, shifted, shifted_twice, shifted_twice], axis=0))
    within = lane % GROUP_SLOTS >= row
    upper = jnp.where(within, packed, mirrored[:small])
    upper = jnp.where(lane < users, upper, 0.0)
    lower = jnp.where((lane >= small) & (lane - small < row), shifted, mirrored[small : 2 * small])
    lower = jnp.where(lane < GROUP_SLOTS, lower, 0.0)
    system = jnp.concatenate([upper, lower], axis=0)
    lane, row = iota(system.shape, 1), iota(system.shape, 0)
    system = jnp.where(lane % GROUP_SLOTS == row, total[gram_rows - 1 : gram_rows] + NOISE_LEVEL, system)
    inverse = invert_pairs(system)
    weights = jnp.concatenate(
        [
            jnp.where(lane < GROUP_SLOTS, inverse, 0.0),
            jnp.where((lane >= GROUP_SLOTS) & (lane < users), inverse, 0.0)[:small],
        ],
        axis=0,
    ).astype(BF16)
    combine = mm(weights, channel).astype(BF16)
    masked = combine * jnp.concatenate([mask] * antennas, axis=1)
    found = mm(masked, data[...]) * estimate_scale
    large_group = found[:GROUP_SLOTS]
    small_group = jnp.concatenate([found[GROUP_SLOTS:], jnp.zeros((GROUP_SLOTS - small, LANES), F32)], axis=0)
    terms[pl.ds(0, GROUP_SLOTS), :] = jnp.where(second_large, small_group, large_group)
    terms[pl.ds(GROUP_SLOTS, GROUP_SLOTS), :] = jnp.where(second_large, large_group, small_group)

    def give(peer):
        make(
            terms.at[pl.ds(peer * out_rows, out_rows)], term_recv.at[me], out_send, out_recv, {"ap": peer}
        ).start()

    pl.loop(0, me)(give)
    pl.loop(me + 1, n)(give)
    term_recv[me] = terms[pl.ds(me * out_rows, out_rows), :]
    shares = term_recv.at[pl.ds(0, n - 1)]
    pltpu.make_async_copy(shares, shares, out_recv).wait()
    out_ref[...] = total_of([term_recv[i] for i in range(n)])
    pltpu.make_async_copy(every, every, gram_send).wait()
    pltpu.make_async_copy(shares, shares, out_send).wait()
    pl.when(has_right)(upward.wait_send)
    pl.when(has_left)(downward.wait_send)


def fused(pilot_received, received, large_scale, pilot_index, serving, user_group):
    n = lax.axis_size("ap")
    sc_count = lax.axis_size("sc")
    _, tau_count, antennas, aps_dev = pilot_received.shape
    symbols = received.shape[3]
    users = pilot_index.shape[0]
    slots = n // 4 * GROUP_SLOTS
    pilot_rows = tau_count * antennas
    out_rows = slots // n
    aps_total = aps_dev * n
    gram_scale = 1.0 / (antennas * aps_total)
    estimate_scale = 1.0 / math.sqrt(antennas * aps_total * serving.shape[1] / users)
    vmem = pl.BlockSpec(memory_space=pltpu.VMEM)
    two = pltpu.SemaphoreType.DMA((2,))
    one = pltpu.SemaphoreType.DMA
    out = pl.pallas_call(
        functools.partial(
            fused_kernel, n, sc_count, users, tau_count, antennas, gram_scale, estimate_scale
        ),
        out_shape=pltpu.VMEM((out_rows, symbols), F32),
        in_specs=[pl.BlockSpec(memory_space=pl.ANY)] * 6,
        out_specs=vmem,
        scratch_shapes=[
            pltpu.VMEM((3 * pilot_rows, aps_dev), BF16),
            pltpu.VMEM((antennas * aps_dev, symbols), BF16),
            pltpu.VMEM((users, aps_dev), BF16),
            pltpu.VMEM((1, users), jnp.int32),
            pltpu.VMEM((serving.shape[1], aps_dev), jnp.int32),
            pltpu.VMEM((1, users), jnp.int32),
            pltpu.VMEM((n, GROUP_SLOTS // 2, LANES), F32),
            pltpu.VMEM((slots, symbols), F32),
            pltpu.VMEM((n, out_rows, symbols), F32),
            pltpu.SemaphoreType.DMA((6,)),
            two, two, one, one, one, one, pltpu.SemaphoreType.REGULAR((n,)), pltpu.SemaphoreType.REGULAR,
        ],
        compiler_params=pltpu.CompilerParams(collective_id=0, has_side_effects=True),
    )(
        pilot_received.reshape(pilot_rows, aps_dev),
        received.reshape(antennas * aps_dev, symbols),
        large_scale,
        pilot_index.reshape(1, users),
        serving.T,
        user_group.reshape(1, users),
    )
    return out.reshape(out_rows, 1, symbols)


def solution(mesh):
    in_specs = (
        P("sc", None, None, "ap"),
        P("sc", None, "ap", None),
        P(None, "ap"),
        P(),
        P("ap", None),
        P(),
    )
    out_specs = P("ap", "sc", None)

    def per_device(*arguments):
        slots = mesh.shape["ap"] // 4 * GROUP_SLOTS
        users = arguments[3].shape[0]
        filled = slots == LANES and 4 * users == 3 * slots
        return (fused if filled else on_device)(*arguments)

    return jax.shard_map(
        per_device, mesh=mesh, in_specs=in_specs, out_specs=out_specs, check_vma=False
    )
```

```python
import functools
import math

import jax
import jax.numpy as jnp
from jax import lax
from jax.experimental import pallas as pl
from jax.experimental.pallas import tpu as pltpu
from jax.sharding import PartitionSpec as P

GROUP_SLOTS = 64


NOISE_LEVEL = 0.05


def extended_2(block, sides, width):
    for axis, dim in sides:
        count = lax.axis_size(axis)
        forward = [(i, i + 1) for i in range(count - 1)]
        backward = [(target, source) for source, target in forward]
        low = lax.ppermute(
            lax.slice_in_dim(block, block.shape[dim] - width, None, axis=dim), axis, forward
        )
        high = lax.ppermute(lax.slice_in_dim(block, 0, width, axis=dim), axis, backward)
        block = jnp.concatenate([low, block, high], axis=dim)
    return block


def slot_tables(pilot_index, user_group, group_count):
    labels = jnp.arange(group_count, dtype=jnp.int32)
    group_hot = (user_group[:, None] == labels[None, :]).astype(jnp.int32)
    users = jnp.arange(user_group.shape[0], dtype=jnp.int32)
    up_to = (users[:, None] >= users[None, :]).astype(jnp.bfloat16)
    counts = jnp.dot(up_to, group_hot.astype(jnp.bfloat16), preferred_element_type=jnp.float32)
    ranks_in = jnp.sum(counts.astype(jnp.int32) * group_hot, axis=1) - 1
    slot_ids = user_group * GROUP_SLOTS + ranks_in
    members = (
        jnp.zeros((group_count * GROUP_SLOTS,), jnp.int32)
        .at[slot_ids]
        .set(jnp.arange(user_group.shape[0], dtype=jnp.int32))
    )
    occupied = jnp.zeros((group_count * GROUP_SLOTS,), jnp.float32).at[slot_ids].set(1.0)
    slot_pilot = pilot_index[members]
    return (members, occupied, slot_pilot)


def inverse_columns(factor, columns):
    first = lax.linalg.triangular_solve(factor, columns, left_side=True, lower=True)
    return lax.linalg.triangular_solve(factor, first, left_side=True, lower=True, transpose_a=True)


def on_device(pilot_received, received, large_scale, pilot_index, serving, user_group):
    ap_count = lax.axis_size("ap")
    sc_count = lax.axis_size("sc")
    ap_index = lax.axis_index("ap")
    sc_index = lax.axis_index("sc")
    blocks_dev, tau_count, antennas, aps_dev = pilot_received.shape
    symbols = received.shape[3]
    users = pilot_index.shape[0]
    serve_count = serving.shape[1]
    groups = ap_count // 4
    quarter = GROUP_SLOTS // 4
    aps_total = aps_dev * ap_count
    members, occupied, slot_pilot = slot_tables(pilot_index, user_group, groups)
    extended = extended_2(pilot_received, (("sc", 0),), 1)
    block_ids = sc_index * blocks_dev + jnp.arange(blocks_dev, dtype=jnp.int32)
    first_block = (block_ids == 0)[:, None, None, None]
    final_block = (block_ids == blocks_dev * sc_count - 1)[:, None, None, None]
    middle = extended[1:-1].astype(jnp.float32)
    before = jnp.where(first_block, middle, extended[:-2].astype(jnp.float32))
    after = jnp.where(final_block, middle, extended[2:].astype(jnp.float32))
    smooth = 0.25 * before + 0.5 * middle + 0.25 * after
    pilot_hot = (pilot_index[None, :] == jnp.arange(tau_count, dtype=jnp.int32)[:, None]).astype(
        jnp.bfloat16
    )
    contamination = 1.0 + tau_count / users * jnp.dot(
        pilot_hot, large_scale, preferred_element_type=jnp.float32
    )
    serve_mask = (
        jnp.zeros((users, aps_dev), jnp.bfloat16)
        .at[serving, jnp.arange(aps_dev, dtype=jnp.int32)[:, None]]
        .set(1.0)
    )
    batch_groups = min(8, groups)
    batches = groups // batch_groups
    batch_rows = batch_groups * GROUP_SLOTS
    member_blocks = members.reshape(batches, batch_rows)
    occupied_blocks = occupied.reshape(batches, batch_rows)
    pilot_blocks = slot_pilot.reshape(batches, batch_rows)
    gramian_scale = 1.0 / (antennas * aps_total)

    def gram_batch(inputs):
        member_rows, occupied_rows, pilot_rows = inputs
        coeff = (
            occupied_rows[:, None]
            * large_scale[member_rows].astype(jnp.float32)
            * lax.rsqrt(contamination[pilot_rows])
        )
        row_hot = (pilot_rows[:, None] == jnp.arange(tau_count, dtype=jnp.int32)).astype(jnp.float32)
        picked = jnp.einsum("st,btnl->bsnl", row_hot, smooth, precision=lax.Precision.HIGHEST)
        channel_gain = (picked * coeff[None, :, None, :]).astype(jnp.bfloat16)
        channel_gain = channel_gain.reshape(
            blocks_dev, batch_groups, GROUP_SLOTS, antennas * aps_dev
        )
        gram = (
            jnp.einsum(
                "bogx,bohx->ogbh", channel_gain, channel_gain, preferred_element_type=jnp.float32
            )
            * gramian_scale
        )
        return (gram, channel_gain)

    partial_gram, channel_store = lax.map(
        gram_batch, (member_blocks, occupied_blocks, pilot_blocks)
    )
    partial_gram = partial_gram.reshape(groups * GROUP_SLOTS, blocks_dev, GROUP_SLOTS)
    summed = lax.psum(partial_gram, "ap")
    owned = lax.dynamic_slice_in_dim(summed, ap_index // 4 * GROUP_SLOTS, GROUP_SLOTS, 0)
    identity = jnp.eye(GROUP_SLOTS, dtype=jnp.float32)
    system = jnp.transpose(owned, (1, 0, 2)) + NOISE_LEVEL * identity
    factor = jnp.linalg.cholesky(system)
    columns = lax.dynamic_slice_in_dim(identity, ap_index % 4 * quarter, quarter, 1)
    solved = inverse_columns(factor, jnp.broadcast_to(columns, (blocks_dev, GROUP_SLOTS, quarter)))
    weight_rows = jnp.transpose(solved, (2, 0, 1)).astype(jnp.bfloat16)
    all_weights = lax.all_gather(weight_rows, "ap", axis=0, tiled=True)
    weight_blocks = all_weights.reshape(batches, batch_groups, GROUP_SLOTS, blocks_dev, GROUP_SLOTS)
    data_signal = received.reshape(blocks_dev, antennas * aps_dev, symbols)
    estimator_scale = 1.0 / math.sqrt(antennas * aps_total * serve_count / users)

    def estimate_batch(inputs):
        member_rows, occupied_rows, channel_gain, weights = inputs
        combiner_weight = jnp.einsum(
            "okbj,bojx->bokx", weights, channel_gain, preferred_element_type=jnp.float32
        ).astype(jnp.bfloat16)
        row_mask_values = serve_mask[member_rows] * occupied_rows[:, None].astype(jnp.bfloat16)
        masked_values = (
            combiner_weight.reshape(blocks_dev, batch_rows, antennas, aps_dev)
            * row_mask_values[None, :, None, :]
        )
        flattened_masked = masked_values.reshape(blocks_dev, batch_rows, antennas * aps_dev)
        return (
            jnp.einsum(
                "bsx,bxt->sbt", flattened_masked, data_signal, preferred_element_type=jnp.float32
            )
            * estimator_scale
        )

    terms = lax.map(estimate_batch, (member_blocks, occupied_blocks, channel_store, weight_blocks))
    terms = terms.reshape(groups * GROUP_SLOTS, blocks_dev, symbols)
    return lax.psum_scatter(terms, "ap", scatter_dimension=0, tiled=True)


LANES = 128
BF16 = jnp.bfloat16
F32 = jnp.float32
NT = (((1,), (1,)), ((), ()))


def iota(shape, dim):
    return lax.broadcasted_iota(jnp.int32, shape, dim)


def mm(a, b, dims=(((1,), (0,)), ((), ()))):
    return lax.dot_general(a, b, dims, preferred_element_type=F32)


def total_of(terms):
    while len(terms) > 1:
        pairs = [a + b for a, b in zip(terms[::2], terms[1::2])]
        terms = pairs + terms[len(terms) // 2 * 2 :]
    return terms[0]


def invert_pairs(mat):
    tile = 8
    inner = iota((tile, LANES), 1) % GROUP_SLOTS
    base = iota((tile, LANES), 1) - inner
    sub = iota((tile, LANES), 0)
    parts = [mat[i : i + tile] for i in range(0, GROUP_SLOTS, tile)]

    def line_of(part, line):
        return jnp.broadcast_to(part[line : line + 1], (tile, LANES))

    for home in range(len(parts)):
        start = home * tile
        rows = parts[home]
        spread = [line_of(rows, k) for k in range(tile)]
        ahead = [jnp.take_along_axis(line, base + start + sub, axis=1) for line in spread]
        columns = [
            [jnp.take_along_axis(line, base + tile * i + sub, axis=1) for line in spread]
            for i in range(len(parts))
        ]
        for j in range(0, tile, 2):
            first, second = ahead[j], ahead[j + 1]
            p00, p01, p11 = line_of(first, j), line_of(second, j), line_of(second, j + 1)
            scale = 1.0 / (p00 * p11 - p01 * p01)
            lines = sub // 2 == j // 2
            first = jnp.where(sub == j, -1.0, jnp.where(sub == j + 1, 0.0, first))
            second = jnp.where(sub == j + 1, -1.0, jnp.where(sub == j, 0.0, second))

            def reduced(kept, upper, lower):
                above, below = p11 * upper - p01 * lower, p00 * lower - p01 * upper
                return kept - (first * above + second * below) * scale

            for k in range(j + 2, tile):
                kept = jnp.where(lines, 0.0, ahead[k])
                ahead[k] = reduced(kept, line_of(ahead[k], j), line_of(ahead[k], j + 1))
            here, there = inner == start + j, inner == start + j + 1
            kept = jnp.where(lines | here | there, 0.0, rows)
            upper = jnp.where(here, 1.0, jnp.where(there, 0.0, line_of(rows, j)))
            lower = jnp.where(there, 1.0, jnp.where(here, 0.0, line_of(rows, j + 1)))
            rows = reduced(kept, upper, lower)
        lines = [line_of(rows, k) for k in range(tile)]
        within = inner // tile == home
        parts = [
            rows
            if i == home
            else (jnp.where(within, 0.0, part) - change if i > home else jnp.where(within, 0.0, part) + change)
            for i, (part, change) in enumerate(
                zip(parts, [total_of([a * b for a, b in zip(column, lines)]) for column in columns])
            )
        ]
    return jnp.concatenate(parts, axis=0)


def fused_kernel(
    n, sc_count, users, tau_count, antennas, gram_scale, estimate_scale,
    pilot_ref, data_ref, large_ref, pilot_index_ref, serving_ref, group_ref,
    out_ref,
    pilots, data, large_in, pilot_index, serving_in, group_in,
    grams, terms, term_recv,
    load, halo_send, halo_recv, gram_send, gram_arrive, out_send, out_recv, ready, side,
):
    me = lax.axis_index("ap")
    sc = lax.axis_index("sc")
    right, left = sc + 1, sc - 1
    pilot_rows = tau_count * antennas
    small = users - GROUP_SLOTS
    out_rows = n // 4 * GROUP_SLOTS // n

    loads = []
    for source, target in (
        (group_ref, group_in), (pilot_index_ref, pilot_index), (large_ref, large_in),
        (pilot_ref, pilots.at[pl.ds(pilot_rows, pilot_rows)]), (serving_ref, serving_in), (data_ref, data),
    ):
        loads.append(pltpu.make_async_copy(source, target, load.at[len(loads)]))
        loads[-1].start()

    def signal(semaphore, **where):
        pl.semaphore_signal(semaphore, inc=1, device_id=where, device_id_type=pl.DeviceIdType.MESH)

    barrier = pltpu.get_barrier_semaphore()
    has_left, has_right = sc > 0, sc < sc_count - 1
    pl.when(has_right)(functools.partial(signal, barrier, sc=right))

    anchors = jnp.where(has_left, 0, n)
    anchor = me < anchors

    @pl.loop(me + 1, n)
    def _(peer):
        signal(barrier, ap=peer)

    @pl.loop(0, jnp.minimum(anchors, me))
    def _(peer):
        signal(barrier, ap=peer)


    def make(src, dst, send_sem, recv_sem, where):
        return pltpu.make_async_remote_copy(
            src_ref=src, dst_ref=dst, send_sem=send_sem, recv_sem=recv_sem,
            device_id=where, device_id_type=pl.DeviceIdType.MESH,
        )

    middle = pilots.at[pl.ds(pilot_rows, pilot_rows)]
    first, last = (pilots.at[pl.ds(i * pilot_rows, pilot_rows)] for i in (0, 2))
    upward = make(middle, first, halo_send.at[0], halo_recv.at[0], {"sc": right})
    downward = make(pilot_ref, last, halo_send.at[1], halo_recv.at[1], {"sc": left})

    def enter():
        pl.semaphore_wait(barrier, has_left.astype(jnp.int32) + jnp.where(anchor, n - 1, me))
        pl.when(has_left)(functools.partial(signal, side, sc=left))
        pl.when(has_left)(downward.start)

        @pl.loop(anchors, me)
        def _(peer):
            signal(ready.at[me], ap=peer)

    pl.when(jnp.logical_not(anchor))(enter)
    blank = jnp.zeros((pilot_rows, pilots.shape[1]), BF16)

    @pl.when(jnp.logical_not(has_left))
    def _():
        pilots[pl.ds(0, pilot_rows), :] = blank

    @pl.when(jnp.logical_not(has_right))
    def _():
        pilots[pl.ds(2 * pilot_rows, pilot_rows), :] = blank

    for copy in loads[:3]:
        copy.wait()
    group = group_in[...]
    wide = (users, 2 * LANES)
    earlier = jnp.where((iota(wide, 0) < iota(wide, 1)) | (iota(wide, 1) >= LANES), 1.0, 0.0)
    counts = mm(jnp.broadcast_to(group, (8, users)).astype(F32).astype(BF16), earlier.astype(BF16))
    later_group = counts[:1, :users].astype(jnp.int32)
    second_large = counts[:1, LANES:] > GROUP_SLOTS - 0.5
    rank = jnp.where(group == 1, later_group, iota(group.shape, 1) - later_group)
    is_large = (group == 1) == second_large[:, :users]
    slot_row = jnp.where(is_large, rank, rank + GROUP_SLOTS)
    hot = jnp.where(iota((users, users), 0) == slot_row, 1.0, 0.0).astype(BF16)
    tall = (LANES, users)
    facts = jnp.concatenate(
        [jnp.broadcast_to(pilot_index[...], tall).astype(F32), iota(tall, 1).astype(F32)], axis=0
    )
    facts = mm(hot, facts.astype(BF16), NT)
    slot_pilot, member = facts[:, :LANES].astype(jnp.int32), facts[:, LANES:].astype(jnp.int32)
    same_pilot = jnp.where(slot_pilot[:, :users] == pilot_index[...], 1.0, 0.0).astype(BF16)
    large = large_in[...]
    contamination = 1.0 + tau_count / users * mm(same_pilot, large)
    coeff = mm(hot, large) * lax.rsqrt(contamination)

    low = jnp.where(sc == 0, 0.0, 0.25)
    high = jnp.where(sc == sc_count - 1, 0.0, 0.25)
    lane = iota((users, LANES), 1)
    meets = slot_pilot == lane % pilot_rows // antennas
    early = jnp.where(meets, jnp.where(lane < pilot_rows, low, 1.0 - low - high), 0.0)
    late = jnp.where(meets, high, 0.0)
    spread = jnp.concatenate(
        [
            jnp.concatenate(
                [
                    jnp.where(lane % antennas == a, early, 0.0).astype(BF16),
                    jnp.where(lane % antennas == a, late, 0.0).astype(BF16)[:, :pilot_rows],
                ],
                axis=1,
            )
            for a in range(antennas)
        ],
        axis=0,
    )

    loads[3].wait()

    @pl.when(has_right)
    def _():
        pl.semaphore_wait(side, 1)
        upward.start()

    pl.when(has_left)(upward.wait_recv)
    pl.when(has_right)(downward.wait_recv)
    smooth = mm(spread, pilots[...])
    channel = jnp.concatenate(
        [(smooth[a * users : (a + 1) * users] * coeff).astype(BF16) for a in range(antennas)], axis=1
    )
    channel = jnp.concatenate([channel, jnp.zeros((LANES - users, channel.shape[1]), BF16)], axis=0)
    gram = mm(channel[:users], channel, NT) * gram_scale

    def turn(part, amount):
        return pltpu.roll(part, amount % LANES, 1)

    lane, row = iota((small, LANES), 1), iota((small, LANES), 0)
    top, bottom, other = (gram[i * small : (i + 1) * small] for i in range(3))
    packed = jnp.where(lane < row, turn(bottom, -small), jnp.where(lane < GROUP_SLOTS, top, other))
    last = packed[small - 8 :]
    eight = iota((8, LANES), 1)
    for i in range(3):
        grams[me, pl.ds(8 * i, 8), :] = jnp.where(
            eight < users, packed[8 * i : 8 * i + 8], turn(last, users - small * i)
        )
    diagonal = [
        jnp.where(lane == row + i * small, part, 0.0) for i, part in enumerate((top, bottom, other))
    ]
    gram_rows = small - 7
    grams[me, pl.ds(gram_rows - 1, 1), :] = jnp.sum(total_of(diagonal), axis=0, keepdims=True)
    own = grams.at[me, pl.ds(0, gram_rows)]
    pl.when(anchor)(enter)

    @pl.loop(0, n - 1)
    def _(i):
        down = n - 1 - i
        peer = jnp.where(anchor, jnp.where(down > me, down, down - 1), jnp.where(i < me, i, i + 1))

        @pl.when(jnp.logical_not(anchor) & (peer > me))
        def _():
            pl.semaphore_wait(ready.at[peer], 1)

        make(own, own, gram_send, gram_arrive, {"ap": peer}).start()

    for copy in loads[4:]:
        copy.wait()
    serving = serving_in[...]
    mask = jnp.zeros((users, serving.shape[1]), F32)
    for j in range(serving.shape[0]):
        mask = jnp.where(member == serving[j : j + 1, :], 1.0, mask)
    mask = mask.astype(BF16)

    every = grams.at[pl.ds(0, n - 1), pl.ds(0, gram_rows)]
    pltpu.make_async_copy(every, every, gram_arrive).wait()
    total = total_of([grams[i, pl.ds(0, gram_rows), :] for i in range(n)])
    parts = [total[8 * i : 8 * i + 8] for i in range(3)]
    last = jnp.where(eight < 2 * small, turn(parts[1], small - users), turn(parts[2], 2 * small - users))
    last = jnp.where(eight < small, turn(parts[0], -users), last)
    packed = jnp.concatenate(parts + [last], axis=0)
    shifted, shifted_twice = turn(packed, small), turn(packed, 2 * small)
    mirrored = jnp.transpose(jnp.concatenate([packed, shifted, shifted_twice, shifted_twice], axis=0))
    within = lane % GROUP_SLOTS >= row
    upper = jnp.where(within, packed, mirrored[:small])
    upper = jnp.where(lane < users, upper, 0.0)
    lower = jnp.where((lane >= small) & (lane - small < row), shifted, mirrored[small : 2 * small])
    lower = jnp.where(lane < GROUP_SLOTS, lower, 0.0)
    system = jnp.concatenate([upper, lower], axis=0)
    lane, row = iota(system.shape, 1), iota(system.shape, 0)
    system = jnp.where(lane % GROUP_SLOTS == row, total[gram_rows - 1 : gram_rows] + NOISE_LEVEL, system)
    inverse = invert_pairs(system)
    weights = jnp.concatenate(
        [
            jnp.where(lane < GROUP_SLOTS, inverse, 0.0),
            jnp.where((lane >= GROUP_SLOTS) & (lane < users), inverse, 0.0)[:small],
        ],
        axis=0,
    ).astype(BF16)
    combine = mm(weights, channel).astype(BF16)
    masked = combine * jnp.concatenate([mask] * antennas, axis=1)
    found = mm(masked, data[...]) * estimate_scale
    large_group = found[:GROUP_SLOTS]
    small_group = jnp.concatenate([found[GROUP_SLOTS:], jnp.zeros((GROUP_SLOTS - small, LANES), F32)], axis=0)
    terms[pl.ds(0, GROUP_SLOTS), :] = jnp.where(second_large, small_group, large_group)
    terms[pl.ds(GROUP_SLOTS, GROUP_SLOTS), :] = jnp.where(second_large, large_group, small_group)

    def give(peer):
        make(
            terms.at[pl.ds(peer * out_rows, out_rows)], term_recv.at[me], out_send, out_recv, {"ap": peer}
        ).start()

    pl.loop(0, me)(give)
    pl.loop(me + 1, n)(give)
    term_recv[me] = terms[pl.ds(me * out_rows, out_rows), :]
    shares = term_recv.at[pl.ds(0, n - 1)]
    pltpu.make_async_copy(shares, shares, out_recv).wait()
    out_ref[...] = total_of([term_recv[i] for i in range(n)])
    pltpu.make_async_copy(every, every, gram_send).wait()
    pltpu.make_async_copy(shares, shares, out_send).wait()
    pl.when(has_right)(upward.wait_send)
    pl.when(has_left)(downward.wait_send)


def fused(pilot_received, received, large_scale, pilot_index, serving, user_group):
    n = lax.axis_size("ap")
    sc_count = lax.axis_size("sc")
    _, tau_count, antennas, aps_dev = pilot_received.shape
    symbols = received.shape[3]
    users = pilot_index.shape[0]
    slots = n // 4 * GROUP_SLOTS
    pilot_rows = tau_count * antennas
    out_rows = slots // n
    aps_total = aps_dev * n
    gram_scale = 1.0 / (antennas * aps_total)
    estimate_scale = 1.0 / math.sqrt(antennas * aps_total * serving.shape[1] / users)
    vmem = pl.BlockSpec(memory_space=pltpu.VMEM)
    two = pltpu.SemaphoreType.DMA((2,))
    one = pltpu.SemaphoreType.DMA
    out = pl.pallas_call(
        functools.partial(
            fused_kernel, n, sc_count, users, tau_count, antennas, gram_scale, estimate_scale
        ),
        out_shape=pltpu.VMEM((out_rows, symbols), F32),
        in_specs=[pl.BlockSpec(memory_space=pl.ANY)] * 6,
        out_specs=vmem,
        scratch_shapes=[
            pltpu.VMEM((3 * pilot_rows, aps_dev), BF16),
            pltpu.VMEM((antennas * aps_dev, symbols), BF16),
            pltpu.VMEM((users, aps_dev), BF16),
            pltpu.VMEM((1, users), jnp.int32),
            pltpu.VMEM((serving.shape[1], aps_dev), jnp.int32),
            pltpu.VMEM((1, users), jnp.int32),
            pltpu.VMEM((n, GROUP_SLOTS // 2, LANES), F32),
            pltpu.VMEM((slots, symbols), F32),
            pltpu.VMEM((n, out_rows, symbols), F32),
            pltpu.SemaphoreType.DMA((6,)),
            two, two, one, one, one, one, pltpu.SemaphoreType.REGULAR((n,)), pltpu.SemaphoreType.REGULAR,
        ],
        compiler_params=pltpu.CompilerParams(collective_id=0, has_side_effects=True),
    )(
        pilot_received.reshape(pilot_rows, aps_dev),
        received.reshape(antennas * aps_dev, symbols),
        large_scale,
        pilot_index.reshape(1, users),
        serving.T,
        user_group.reshape(1, users),
    )
    return out.reshape(out_rows, 1, symbols)


def solution(mesh):
    in_specs = (
        P("sc", None, None, "ap"),
        P("sc", None, "ap", None),
        P(None, "ap"),
        P(),
        P("ap", None),
        P(),
    )
    out_specs = P("ap", "sc", None)

    def per_device(*arguments):
        slots = mesh.shape["ap"] // 4 * GROUP_SLOTS
        users = arguments[3].shape[0]
        filled = slots == LANES and 4 * users == 3 * slots
        return (fused if filled else on_device)(*arguments)

    return jax.shard_map(
        per_device, mesh=mesh, in_specs=in_specs, out_specs=out_specs, check_vma=False
    )
```

```python
import functools
import math

import jax
import jax.numpy as jnp
from jax import lax
from jax.experimental import pallas as pl
from jax.experimental.pallas import tpu as pltpu
from jax.sharding import PartitionSpec as P

GROUP_SLOTS = 64


NOISE_LEVEL = 0.05


def extended_2(block, sides, width):
    for axis, dim in sides:
        count = lax.axis_size(axis)
        forward = [(i, i + 1) for i in range(count - 1)]
        backward = [(target, source) for source, target in forward]
        low = lax.ppermute(
            lax.slice_in_dim(block, block.shape[dim] - width, None, axis=dim), axis, forward
        )
        high = lax.ppermute(lax.slice_in_dim(block, 0, width, axis=dim), axis, backward)
        block = jnp.concatenate([low, block, high], axis=dim)
    return block


def slot_tables(pilot_index, user_group, group_count):
    labels = jnp.arange(group_count, dtype=jnp.int32)
    group_hot = (user_group[:, None] == labels[None, :]).astype(jnp.int32)
    users = jnp.arange(user_group.shape[0], dtype=jnp.int32)
    up_to = (users[:, None] >= users[None, :]).astype(jnp.bfloat16)
    counts = jnp.dot(up_to, group_hot.astype(jnp.bfloat16), preferred_element_type=jnp.float32)
    ranks_in = jnp.sum(counts.astype(jnp.int32) * group_hot, axis=1) - 1
    slot_ids = user_group * GROUP_SLOTS + ranks_in
    members = (
        jnp.zeros((group_count * GROUP_SLOTS,), jnp.int32)
        .at[slot_ids]
        .set(jnp.arange(user_group.shape[0], dtype=jnp.int32))
    )
    occupied = jnp.zeros((group_count * GROUP_SLOTS,), jnp.float32).at[slot_ids].set(1.0)
    slot_pilot = pilot_index[members]
    return (members, occupied, slot_pilot)


def inverse_columns(factor, columns):
    first = lax.linalg.triangular_solve(factor, columns, left_side=True, lower=True)
    return lax.linalg.triangular_solve(factor, first, left_side=True, lower=True, transpose_a=True)


def on_device(pilot_received, received, large_scale, pilot_index, serving, user_group):
    ap_count = lax.axis_size("ap")
    sc_count = lax.axis_size("sc")
    ap_index = lax.axis_index("ap")
    sc_index = lax.axis_index("sc")
    blocks_dev, tau_count, antennas, aps_dev = pilot_received.shape
    symbols = received.shape[3]
    users = pilot_index.shape[0]
    serve_count = serving.shape[1]
    groups = ap_count // 4
    quarter = GROUP_SLOTS // 4
    aps_total = aps_dev * ap_count
    members, occupied, slot_pilot = slot_tables(pilot_index, user_group, groups)
    extended = extended_2(pilot_received, (("sc", 0),), 1)
    block_ids = sc_index * blocks_dev + jnp.arange(blocks_dev, dtype=jnp.int32)
    first_block = (block_ids == 0)[:, None, None, None]
    final_block = (block_ids == blocks_dev * sc_count - 1)[:, None, None, None]
    middle = extended[1:-1].astype(jnp.float32)
    before = jnp.where(first_block, middle, extended[:-2].astype(jnp.float32))
    after = jnp.where(final_block, middle, extended[2:].astype(jnp.float32))
    smooth = 0.25 * before + 0.5 * middle + 0.25 * after
    pilot_hot = (pilot_index[None, :] == jnp.arange(tau_count, dtype=jnp.int32)[:, None]).astype(
        jnp.bfloat16
    )
    contamination = 1.0 + tau_count / users * jnp.dot(
        pilot_hot, large_scale, preferred_element_type=jnp.float32
    )
    serve_mask = (
        jnp.zeros((users, aps_dev), jnp.bfloat16)
        .at[serving, jnp.arange(aps_dev, dtype=jnp.int32)[:, None]]
        .set(1.0)
    )
    batch_groups = min(8, groups)
    batches = groups // batch_groups
    batch_rows = batch_groups * GROUP_SLOTS
    member_blocks = members.reshape(batches, batch_rows)
    occupied_blocks = occupied.reshape(batches, batch_rows)
    pilot_blocks = slot_pilot.reshape(batches, batch_rows)
    gramian_scale = 1.0 / (antennas * aps_total)

    def gram_batch(inputs):
        member_rows, occupied_rows, pilot_rows = inputs
        coeff = (
            occupied_rows[:, None]
            * large_scale[member_rows].astype(jnp.float32)
            * lax.rsqrt(contamination[pilot_rows])
        )
        row_hot = (pilot_rows[:, None] == jnp.arange(tau_count, dtype=jnp.int32)).astype(jnp.float32)
        picked = jnp.einsum("st,btnl->bsnl", row_hot, smooth, precision=lax.Precision.HIGHEST)
        channel_gain = (picked * coeff[None, :, None, :]).astype(jnp.bfloat16)
        channel_gain = channel_gain.reshape(
            blocks_dev, batch_groups, GROUP_SLOTS, antennas * aps_dev
        )
        gram = (
            jnp.einsum(
                "bogx,bohx->ogbh", channel_gain, channel_gain, preferred_element_type=jnp.float32
            )
            * gramian_scale
        )
        return (gram, channel_gain)

    partial_gram, channel_store = lax.map(
        gram_batch, (member_blocks, occupied_blocks, pilot_blocks)
    )
    partial_gram = partial_gram.reshape(groups * GROUP_SLOTS, blocks_dev, GROUP_SLOTS)
    summed = lax.psum(partial_gram, "ap")
    owned = lax.dynamic_slice_in_dim(summed, ap_index // 4 * GROUP_SLOTS, GROUP_SLOTS, 0)
    identity = jnp.eye(GROUP_SLOTS, dtype=jnp.float32)
    system = jnp.transpose(owned, (1, 0, 2)) + NOISE_LEVEL * identity
    factor = jnp.linalg.cholesky(system)
    columns = lax.dynamic_slice_in_dim(identity, ap_index % 4 * quarter, quarter, 1)
    solved = inverse_columns(factor, jnp.broadcast_to(columns, (blocks_dev, GROUP_SLOTS, quarter)))
    weight_rows = jnp.transpose(solved, (2, 0, 1)).astype(jnp.bfloat16)
    all_weights = lax.all_gather(weight_rows, "ap", axis=0, tiled=True)
    weight_blocks = all_weights.reshape(batches, batch_groups, GROUP_SLOTS, blocks_dev, GROUP_SLOTS)
    data_signal = received.reshape(blocks_dev, antennas * aps_dev, symbols)
    estimator_scale = 1.0 / math.sqrt(antennas * aps_total * serve_count / users)

    def estimate_batch(inputs):
        member_rows, occupied_rows, channel_gain, weights = inputs
        combiner_weight = jnp.einsum(
            "okbj,bojx->bokx", weights, channel_gain, preferred_element_type=jnp.float32
        ).astype(jnp.bfloat16)
        row_mask_values = serve_mask[member_rows] * occupied_rows[:, None].astype(jnp.bfloat16)
        masked_values = (
            combiner_weight.reshape(blocks_dev, batch_rows, antennas, aps_dev)
            * row_mask_values[None, :, None, :]
        )
        flattened_masked = masked_values.reshape(blocks_dev, batch_rows, antennas * aps_dev)
        return (
            jnp.einsum(
                "bsx,bxt->sbt", flattened_masked, data_signal, preferred_element_type=jnp.float32
            )
            * estimator_scale
        )

    terms = lax.map(estimate_batch, (member_blocks, occupied_blocks, channel_store, weight_blocks))
    terms = terms.reshape(groups * GROUP_SLOTS, blocks_dev, symbols)
    return lax.psum_scatter(terms, "ap", scatter_dimension=0, tiled=True)


LANES = 128
BF16 = jnp.bfloat16
F32 = jnp.float32
NT = (((1,), (1,)), ((), ()))


def iota(shape, dim):
    return lax.broadcasted_iota(jnp.int32, shape, dim)


def mm(a, b, dims=(((1,), (0,)), ((), ()))):
    return lax.dot_general(a, b, dims, preferred_element_type=F32)


def total_of(terms):
    while len(terms) > 1:
        pairs = [a + b for a, b in zip(terms[::2], terms[1::2])]
        terms = pairs + terms[len(terms) // 2 * 2 :]
    return terms[0]


def invert_pairs(mat):
    tile = 8
    inner = iota((tile, LANES), 1) % GROUP_SLOTS
    base = iota((tile, LANES), 1) - inner
    sub = iota((tile, LANES), 0)
    parts = [mat[i : i + tile] for i in range(0, GROUP_SLOTS, tile)]

    def line_of(part, line):
        return jnp.broadcast_to(part[line : line + 1], (tile, LANES))

    for home in range(len(parts)):
        start = home * tile
        rows = parts[home]
        spread = [line_of(rows, k) for k in range(tile)]
        ahead = [jnp.take_along_axis(line, base + start + sub, axis=1) for line in spread]
        columns = [
            [jnp.take_along_axis(line, base + tile * i + sub, axis=1) for line in spread]
            for i in range(len(parts))
        ]
        for j in range(0, tile, 2):
            first, second = ahead[j], ahead[j + 1]
            p00, p01, p11 = line_of(first, j), line_of(second, j), line_of(second, j + 1)
            scale = 1.0 / (p00 * p11 - p01 * p01)
            lines = sub // 2 == j // 2
            first = jnp.where(sub == j, -1.0, jnp.where(sub == j + 1, 0.0, first))
            second = jnp.where(sub == j + 1, -1.0, jnp.where(sub == j, 0.0, second))

            def reduced(kept, upper, lower):
                above, below = p11 * upper - p01 * lower, p00 * lower - p01 * upper
                return kept - (first * above + second * below) * scale

            for k in range(j + 2, tile):
                kept = jnp.where(lines, 0.0, ahead[k])
                ahead[k] = reduced(kept, line_of(ahead[k], j), line_of(ahead[k], j + 1))
            here, there = inner == start + j, inner == start + j + 1
            kept = jnp.where(lines | here | there, 0.0, rows)
            upper = jnp.where(here, 1.0, jnp.where(there, 0.0, line_of(rows, j)))
            lower = jnp.where(there, 1.0, jnp.where(here, 0.0, line_of(rows, j + 1)))
            rows = reduced(kept, upper, lower)
        lines = [line_of(rows, k) for k in range(tile)]
        within = inner // tile == home
        parts = [
            rows
            if i == home
            else (jnp.where(within, 0.0, part) - change if i > home else jnp.where(within, 0.0, part) + change)
            for i, (part, change) in enumerate(
                zip(parts, [total_of([a * b for a, b in zip(column, lines)]) for column in columns])
            )
        ]
    return jnp.concatenate(parts, axis=0)


def fused_kernel(
    n, sc_count, users, tau_count, antennas, gram_scale, estimate_scale,
    pilot_ref, data_ref, large_ref, pilot_index_ref, serving_ref, group_ref,
    out_ref,
    pilots, data, large_in, pilot_index, serving_in, group_in,
    grams, terms, term_recv,
    load, halo_send, halo_recv, gram_send, gram_arrive, given_send, given_arrive, out_send, out_recv, ready, side,
):
    me = lax.axis_index("ap")
    sc = lax.axis_index("sc")
    right, left = sc + 1, sc - 1
    pilot_rows = tau_count * antennas
    small = users - GROUP_SLOTS
    out_rows = n // 4 * GROUP_SLOTS // n

    loads = []
    for source, target in (
        (group_ref, group_in), (pilot_index_ref, pilot_index), (large_ref, large_in),
        (pilot_ref, pilots.at[pl.ds(pilot_rows, pilot_rows)]), (serving_ref, serving_in), (data_ref, data),
    ):
        loads.append(pltpu.make_async_copy(source, target, load.at[len(loads)]))
        loads[-1].start()

    def signal(semaphore, **where):
        pl.semaphore_signal(semaphore, inc=1, device_id=where, device_id_type=pl.DeviceIdType.MESH)

    barrier = pltpu.get_barrier_semaphore()
    has_left, has_right = sc > 0, sc < sc_count - 1
    pl.when(has_right)(functools.partial(signal, barrier, sc=right))

    anchors = jnp.where(has_left, 0, n)
    anchor = me < anchors
    giver, taker = anchor & (me == 0), anchor & (me == 1)
    hubbed = sc == sc_count - 2
    is_hub = (me == n // 2) & (sc == sc_count - 1)
    pl.when(hubbed)(functools.partial(signal, barrier, ap=n // 2, sc=right))

    @pl.loop(jnp.where(hubbed, n, me + 1), n)
    def _(peer):
        signal(barrier, ap=peer)

    @pl.loop(jnp.where(me > 1, 1, 0), jnp.minimum(anchors, me))
    def _(peer):
        signal(barrier, ap=peer)


    def make(src, dst, send_sem, recv_sem, where):
        return pltpu.make_async_remote_copy(
            src_ref=src, dst_ref=dst, send_sem=send_sem, recv_sem=recv_sem,
            device_id=where, device_id_type=pl.DeviceIdType.MESH,
        )

    middle = pilots.at[pl.ds(pilot_rows, pilot_rows)]
    first, last = (pilots.at[pl.ds(i * pilot_rows, pilot_rows)] for i in (0, 2))
    upward = make(middle, first, halo_send.at[0], halo_recv.at[0], {"sc": right})
    downward = make(pilot_ref, last, halo_send.at[1], halo_recv.at[1], {"sc": left})

    def enter():
        peers = jnp.where(anchor, jnp.where(giver, 1, n - 1), jnp.where(hubbed, 0, me)) + jnp.where(is_hub, n, 0)
        pl.semaphore_wait(barrier, has_left.astype(jnp.int32) + peers)
        pl.when(has_left)(functools.partial(signal, side, sc=left))
        pl.when(has_left)(downward.start)

        @pl.loop(jnp.where(hubbed, me, anchors), me)
        def _(peer):
            signal(ready.at[me], ap=peer)

        @pl.loop(0, jnp.where(is_hub, n, 0))
        def _(peer):
            signal(ready.at[0], ap=peer, sc=left)

    pl.when(jnp.logical_not(anchor))(enter)
    @pl.when(anchor & (me > 1))
    def _():
        grams[0] = jnp.zeros(grams.shape[1:], F32)

    blank = jnp.zeros((pilot_rows, pilots.shape[1]), BF16)

    @pl.when(jnp.logical_not(has_left))
    def _():
        pilots[pl.ds(0, pilot_rows), :] = blank

    @pl.when(jnp.logical_not(has_right))
    def _():
        pilots[pl.ds(2 * pilot_rows, pilot_rows), :] = blank

    for copy in loads[:3]:
        copy.wait()
    group = group_in[...]
    wide = (users, 2 * LANES)
    earlier = jnp.where((iota(wide, 0) < iota(wide, 1)) | (iota(wide, 1) >= LANES), 1.0, 0.0)
    counts = mm(jnp.broadcast_to(group, (8, users)).astype(F32).astype(BF16), earlier.astype(BF16))
    later_group = counts[:1, :users].astype(jnp.int32)
    second_large = counts[:1, LANES:] > GROUP_SLOTS - 0.5
    rank = jnp.where(group == 1, later_group, iota(group.shape, 1) - later_group)
    is_large = (group == 1) == second_large[:, :users]
    slot_row = jnp.where(is_large, rank, rank + GROUP_SLOTS)
    hot = jnp.where(iota((users, users), 0) == slot_row, 1.0, 0.0).astype(BF16)
    tall = (LANES, users)
    facts = jnp.concatenate(
        [jnp.broadcast_to(pilot_index[...], tall).astype(F32), iota(tall, 1).astype(F32)], axis=0
    )
    facts = mm(hot, facts.astype(BF16), NT)
    slot_pilot, member = facts[:, :LANES].astype(jnp.int32), facts[:, LANES:].astype(jnp.int32)
    same_pilot = jnp.where(slot_pilot[:, :users] == pilot_index[...], 1.0, 0.0).astype(BF16)
    large = large_in[...]
    contamination = 1.0 + tau_count / users * mm(same_pilot, large)
    coeff = mm(hot, large) * lax.rsqrt(contamination)

    low = jnp.where(sc == 0, 0.0, 0.25)
    high = jnp.where(sc == sc_count - 1, 0.0, 0.25)
    lane = iota((users, LANES), 1)
    meets = slot_pilot == lane % pilot_rows // antennas
    early = jnp.where(meets, jnp.where(lane < pilot_rows, low, 1.0 - low - high), 0.0)
    late = jnp.where(meets, high, 0.0)
    spread = jnp.concatenate(
        [
            jnp.concatenate(
                [
                    jnp.where(lane % antennas == a, early, 0.0).astype(BF16),
                    jnp.where(lane % antennas == a, late, 0.0).astype(BF16)[:, :pilot_rows],
                ],
                axis=1,
            )
            for a in range(antennas)
        ],
        axis=0,
    )

    loads[3].wait()

    @pl.when(has_right)
    def _():
        pl.semaphore_wait(side, 1)
        upward.start()

    pl.when(has_left)(upward.wait_recv)
    pl.when(has_right)(downward.wait_recv)
    smooth = mm(spread, pilots[...])
    channel = jnp.concatenate(
        [(smooth[a * users : (a + 1) * users] * coeff).astype(BF16) for a in range(antennas)], axis=1
    )
    channel = jnp.concatenate([channel, jnp.zeros((LANES - users, channel.shape[1]), BF16)], axis=0)
    gram = mm(channel[:users], channel, NT) * gram_scale

    def turn(part, amount):
        return pltpu.roll(part, amount % LANES, 1)

    lane, row = iota((small, LANES), 1), iota((small, LANES), 0)
    top, bottom, other = (gram[i * small : (i + 1) * small] for i in range(3))
    packed = jnp.where(lane < row, turn(bottom, -small), jnp.where(lane < GROUP_SLOTS, top, other))
    last = packed[small - 8 :]
    eight = iota((8, LANES), 1)
    for i in range(3):
        grams[me, pl.ds(8 * i, 8), :] = jnp.where(
            eight < users, packed[8 * i : 8 * i + 8], turn(last, users - small * i)
        )
    diagonal = [
        jnp.where(lane == row + i * small, part, 0.0) for i, part in enumerate((top, bottom, other))
    ]
    gram_rows = small - 7
    grams[me, pl.ds(gram_rows - 1, 1), :] = jnp.sum(total_of(diagonal), axis=0, keepdims=True)
    own = grams.at[me, pl.ds(0, gram_rows)]
    pl.when(anchor)(enter)
    given = grams.at[0, pl.ds(0, gram_rows)]
    gift = make(given, given, given_send, given_arrive, {"ap": 1})
    pl.when(giver)(gift.start)

    @pl.when(taker)
    def _():
        gift.wait_recv()
        grams[1, pl.ds(0, gram_rows), :] += grams[0, pl.ds(0, gram_rows), :]

    @pl.when(hubbed)
    def _():
        pl.semaphore_wait(ready.at[0], 1)

    known = anchor | hubbed

    @pl.loop(0, jnp.where(giver, 0, n - 1))
    def _(i):
        down = n - 1 - i
        peer = jnp.where(known, jnp.where(down > me, down, down - 1), jnp.where(i < me, i, i + 1))

        @pl.when(jnp.logical_not(known) & (peer > me))
        def _():
            pl.semaphore_wait(ready.at[peer], 1)

        make(own, own, gram_send, gram_arrive, {"ap": peer}).start()

    for copy in loads[4:]:
        copy.wait()
    serving = serving_in[...]
    mask = jnp.zeros((users, serving.shape[1]), F32)
    for j in range(serving.shape[0]):
        mask = jnp.where(member == serving[j : j + 1, :], 1.0, mask)
    mask = mask.astype(BF16)

    every = grams.at[pl.ds(0, n - 1), pl.ds(0, gram_rows)]
    fewer = grams.at[pl.ds(0, n - 2), pl.ds(0, gram_rows)]
    direct = jnp.logical_not(anchor) | giver
    pl.when(direct)(pltpu.make_async_copy(every, every, gram_arrive).wait)
    pl.when(jnp.logical_not(direct))(pltpu.make_async_copy(fewer, fewer, gram_arrive).wait)
    total = [grams[i, pl.ds(0, gram_rows), :] for i in range(n)]
    total = total_of([jnp.where(anchor, 0.0, total[0])] + total[1:])
    parts = [total[8 * i : 8 * i + 8] for i in range(3)]
    last = jnp.where(eight < 2 * small, turn(parts[1], small - users), turn(parts[2], 2 * small - users))
    last = jnp.where(eight < small, turn(parts[0], -users), last)
    packed = jnp.concatenate(parts + [last], axis=0)
    shifted, shifted_twice = turn(packed, small), turn(packed, 2 * small)
    mirrored = jnp.transpose(jnp.concatenate([packed, shifted, shifted_twice, shifted_twice], axis=0))
    within = lane % GROUP_SLOTS >= row
    upper = jnp.where(within, packed, mirrored[:small])
    upper = jnp.where(lane < users, upper, 0.0)
    lower = jnp.where((lane >= small) & (lane - small < row), shifted, mirrored[small : 2 * small])
    lower = jnp.where(lane < GROUP_SLOTS, lower, 0.0)
    system = jnp.concatenate([upper, lower], axis=0)
    lane, row = iota(system.shape, 1), iota(system.shape, 0)
    system = jnp.where(lane % GROUP_SLOTS == row, total[gram_rows - 1 : gram_rows] + NOISE_LEVEL, system)
    inverse = invert_pairs(system)
    weights = jnp.concatenate(
        [
            jnp.where(lane < GROUP_SLOTS, inverse, 0.0),
            jnp.where((lane >= GROUP_SLOTS) & (lane < users), inverse, 0.0)[:small],
        ],
        axis=0,
    ).astype(BF16)
    combine = mm(weights, channel).astype(BF16)
    masked = combine * jnp.concatenate([mask] * antennas, axis=1)
    found = mm(masked, data[...]) * estimate_scale
    large_group = found[:GROUP_SLOTS]
    small_group = jnp.concatenate([found[GROUP_SLOTS:], jnp.zeros((GROUP_SLOTS - small, LANES), F32)], axis=0)
    terms[pl.ds(0, GROUP_SLOTS), :] = jnp.where(second_large, small_group, large_group)
    terms[pl.ds(GROUP_SLOTS, GROUP_SLOTS), :] = jnp.where(second_large, large_group, small_group)

    def give(peer):
        make(
            terms.at[pl.ds(peer * out_rows, out_rows)], term_recv.at[me], out_send, out_recv, {"ap": peer}
        ).start()

    pl.loop(0, me)(give)
    pl.loop(me + 1, n)(give)
    term_recv[me] = terms[pl.ds(me * out_rows, out_rows), :]
    shares = term_recv.at[pl.ds(0, n - 1)]
    pltpu.make_async_copy(shares, shares, out_recv).wait()
    out_ref[...] = total_of([term_recv[i] for i in range(n)])
    pl.when(giver)(gift.wait_send)
    pl.when(jnp.logical_not(giver))(pltpu.make_async_copy(every, every, gram_send).wait)
    pltpu.make_async_copy(shares, shares, out_send).wait()
    pl.when(has_right)(upward.wait_send)
    pl.when(has_left)(downward.wait_send)


def fused(pilot_received, received, large_scale, pilot_index, serving, user_group):
    n = lax.axis_size("ap")
    sc_count = lax.axis_size("sc")
    _, tau_count, antennas, aps_dev = pilot_received.shape
    symbols = received.shape[3]
    users = pilot_index.shape[0]
    slots = n // 4 * GROUP_SLOTS
    pilot_rows = tau_count * antennas
    out_rows = slots // n
    aps_total = aps_dev * n
    gram_scale = 1.0 / (antennas * aps_total)
    estimate_scale = 1.0 / math.sqrt(antennas * aps_total * serving.shape[1] / users)
    vmem = pl.BlockSpec(memory_space=pltpu.VMEM)
    two = pltpu.SemaphoreType.DMA((2,))
    one = pltpu.SemaphoreType.DMA
    out = pl.pallas_call(
        functools.partial(
            fused_kernel, n, sc_count, users, tau_count, antennas, gram_scale, estimate_scale
        ),
        out_shape=pltpu.VMEM((out_rows, symbols), F32),
        in_specs=[pl.BlockSpec(memory_space=pl.ANY)] * 6,
        out_specs=vmem,
        scratch_shapes=[
            pltpu.VMEM((3 * pilot_rows, aps_dev), BF16),
            pltpu.VMEM((antennas * aps_dev, symbols), BF16),
            pltpu.VMEM((users, aps_dev), BF16),
            pltpu.VMEM((1, users), jnp.int32),
            pltpu.VMEM((serving.shape[1], aps_dev), jnp.int32),
            pltpu.VMEM((1, users), jnp.int32),
            pltpu.VMEM((n, GROUP_SLOTS // 2, LANES), F32),
            pltpu.VMEM((slots, symbols), F32),
            pltpu.VMEM((n, out_rows, symbols), F32),
            pltpu.SemaphoreType.DMA((6,)),
            two, two, one, one, one, one, one, one, pltpu.SemaphoreType.REGULAR((n,)), pltpu.SemaphoreType.REGULAR,
        ],
        compiler_params=pltpu.CompilerParams(collective_id=0, has_side_effects=True),
    )(
        pilot_received.reshape(pilot_rows, aps_dev),
        received.reshape(antennas * aps_dev, symbols),
        large_scale,
        pilot_index.reshape(1, users),
        serving.T,
        user_group.reshape(1, users),
    )
    return out.reshape(out_rows, 1, symbols)


def solution(mesh):
    in_specs = (
        P("sc", None, None, "ap"),
        P("sc", None, "ap", None),
        P(None, "ap"),
        P(),
        P("ap", None),
        P(),
    )
    out_specs = P("ap", "sc", None)

    def per_device(*arguments):
        slots = mesh.shape["ap"] // 4 * GROUP_SLOTS
        users = arguments[3].shape[0]
        filled = slots == LANES and 4 * users == 3 * slots and mesh.shape["sc"] > 2
        return (fused if filled else on_device)(*arguments)

    return jax.shard_map(
        per_device, mesh=mesh, in_specs=in_specs, out_specs=out_specs, check_vma=False
    )
```

```python
import functools
import math

import jax
import jax.numpy as jnp
from jax import lax
from jax.experimental import pallas as pl
from jax.experimental.pallas import tpu as pltpu
from jax.sharding import PartitionSpec as P

GROUP_SLOTS = 64


NOISE_LEVEL = 0.05


def extended_2(block, sides, width):
    for axis, dim in sides:
        count = lax.axis_size(axis)
        forward = [(i, i + 1) for i in range(count - 1)]
        backward = [(target, source) for source, target in forward]
        low = lax.ppermute(
            lax.slice_in_dim(block, block.shape[dim] - width, None, axis=dim), axis, forward
        )
        high = lax.ppermute(lax.slice_in_dim(block, 0, width, axis=dim), axis, backward)
        block = jnp.concatenate([low, block, high], axis=dim)
    return block


def slot_tables(pilot_index, user_group, group_count):
    labels = jnp.arange(group_count, dtype=jnp.int32)
    group_hot = (user_group[:, None] == labels[None, :]).astype(jnp.int32)
    users = jnp.arange(user_group.shape[0], dtype=jnp.int32)
    up_to = (users[:, None] >= users[None, :]).astype(jnp.bfloat16)
    counts = jnp.dot(up_to, group_hot.astype(jnp.bfloat16), preferred_element_type=jnp.float32)
    ranks_in = jnp.sum(counts.astype(jnp.int32) * group_hot, axis=1) - 1
    slot_ids = user_group * GROUP_SLOTS + ranks_in
    members = (
        jnp.zeros((group_count * GROUP_SLOTS,), jnp.int32)
        .at[slot_ids]
        .set(jnp.arange(user_group.shape[0], dtype=jnp.int32))
    )
    occupied = jnp.zeros((group_count * GROUP_SLOTS,), jnp.float32).at[slot_ids].set(1.0)
    slot_pilot = pilot_index[members]
    return (members, occupied, slot_pilot)


def inverse_columns(factor, columns):
    first = lax.linalg.triangular_solve(factor, columns, left_side=True, lower=True)
    return lax.linalg.triangular_solve(factor, first, left_side=True, lower=True, transpose_a=True)


def on_device(pilot_received, received, large_scale, pilot_index, serving, user_group):
    ap_count = lax.axis_size("ap")
    sc_count = lax.axis_size("sc")
    ap_index = lax.axis_index("ap")
    sc_index = lax.axis_index("sc")
    blocks_dev, tau_count, antennas, aps_dev = pilot_received.shape
    symbols = received.shape[3]
    users = pilot_index.shape[0]
    serve_count = serving.shape[1]
    groups = ap_count // 4
    quarter = GROUP_SLOTS // 4
    aps_total = aps_dev * ap_count
    members, occupied, slot_pilot = slot_tables(pilot_index, user_group, groups)
    extended = extended_2(pilot_received, (("sc", 0),), 1)
    block_ids = sc_index * blocks_dev + jnp.arange(blocks_dev, dtype=jnp.int32)
    first_block = (block_ids == 0)[:, None, None, None]
    final_block = (block_ids == blocks_dev * sc_count - 1)[:, None, None, None]
    middle = extended[1:-1].astype(jnp.float32)
    before = jnp.where(first_block, middle, extended[:-2].astype(jnp.float32))
    after = jnp.where(final_block, middle, extended[2:].astype(jnp.float32))
    smooth = 0.25 * before + 0.5 * middle + 0.25 * after
    pilot_hot = (pilot_index[None, :] == jnp.arange(tau_count, dtype=jnp.int32)[:, None]).astype(
        jnp.bfloat16
    )
    contamination = 1.0 + tau_count / users * jnp.dot(
        pilot_hot, large_scale, preferred_element_type=jnp.float32
    )
    serve_mask = (
        jnp.zeros((users, aps_dev), jnp.bfloat16)
        .at[serving, jnp.arange(aps_dev, dtype=jnp.int32)[:, None]]
        .set(1.0)
    )
    batch_groups = min(8, groups)
    batches = groups // batch_groups
    batch_rows = batch_groups * GROUP_SLOTS
    member_blocks = members.reshape(batches, batch_rows)
    occupied_blocks = occupied.reshape(batches, batch_rows)
    pilot_blocks = slot_pilot.reshape(batches, batch_rows)
    gramian_scale = 1.0 / (antennas * aps_total)

    def gram_batch(inputs):
        member_rows, occupied_rows, pilot_rows = inputs
        coeff = (
            occupied_rows[:, None]
            * large_scale[member_rows].astype(jnp.float32)
            * lax.rsqrt(contamination[pilot_rows])
        )
        row_hot = (pilot_rows[:, None] == jnp.arange(tau_count, dtype=jnp.int32)).astype(jnp.float32)
        picked = jnp.einsum("st,btnl->bsnl", row_hot, smooth, precision=lax.Precision.HIGHEST)
        channel_gain = (picked * coeff[None, :, None, :]).astype(jnp.bfloat16)
        channel_gain = channel_gain.reshape(
            blocks_dev, batch_groups, GROUP_SLOTS, antennas * aps_dev
        )
        gram = (
            jnp.einsum(
                "bogx,bohx->ogbh", channel_gain, channel_gain, preferred_element_type=jnp.float32
            )
            * gramian_scale
        )
        return (gram, channel_gain)

    partial_gram, channel_store = lax.map(
        gram_batch, (member_blocks, occupied_blocks, pilot_blocks)
    )
    partial_gram = partial_gram.reshape(groups * GROUP_SLOTS, blocks_dev, GROUP_SLOTS)
    summed = lax.psum(partial_gram, "ap")
    owned = lax.dynamic_slice_in_dim(summed, ap_index // 4 * GROUP_SLOTS, GROUP_SLOTS, 0)
    identity = jnp.eye(GROUP_SLOTS, dtype=jnp.float32)
    system = jnp.transpose(owned, (1, 0, 2)) + NOISE_LEVEL * identity
    factor = jnp.linalg.cholesky(system)
    columns = lax.dynamic_slice_in_dim(identity, ap_index % 4 * quarter, quarter, 1)
    solved = inverse_columns(factor, jnp.broadcast_to(columns, (blocks_dev, GROUP_SLOTS, quarter)))
    weight_rows = jnp.transpose(solved, (2, 0, 1)).astype(jnp.bfloat16)
    all_weights = lax.all_gather(weight_rows, "ap", axis=0, tiled=True)
    weight_blocks = all_weights.reshape(batches, batch_groups, GROUP_SLOTS, blocks_dev, GROUP_SLOTS)
    data_signal = received.reshape(blocks_dev, antennas * aps_dev, symbols)
    estimator_scale = 1.0 / math.sqrt(antennas * aps_total * serve_count / users)

    def estimate_batch(inputs):
        member_rows, occupied_rows, channel_gain, weights = inputs
        combiner_weight = jnp.einsum(
            "okbj,bojx->bokx", weights, channel_gain, preferred_element_type=jnp.float32
        ).astype(jnp.bfloat16)
        row_mask_values = serve_mask[member_rows] * occupied_rows[:, None].astype(jnp.bfloat16)
        masked_values = (
            combiner_weight.reshape(blocks_dev, batch_rows, antennas, aps_dev)
            * row_mask_values[None, :, None, :]
        )
        flattened_masked = masked_values.reshape(blocks_dev, batch_rows, antennas * aps_dev)
        return (
            jnp.einsum(
                "bsx,bxt->sbt", flattened_masked, data_signal, preferred_element_type=jnp.float32
            )
            * estimator_scale
        )

    terms = lax.map(estimate_batch, (member_blocks, occupied_blocks, channel_store, weight_blocks))
    terms = terms.reshape(groups * GROUP_SLOTS, blocks_dev, symbols)
    return lax.psum_scatter(terms, "ap", scatter_dimension=0, tiled=True)


LANES = 128
BF16 = jnp.bfloat16
F32 = jnp.float32
NT = (((1,), (1,)), ((), ()))


def iota(shape, dim):
    return lax.broadcasted_iota(jnp.int32, shape, dim)


def mm(a, b, dims=(((1,), (0,)), ((), ()))):
    return lax.dot_general(a, b, dims, preferred_element_type=F32)


def total_of(terms):
    while len(terms) > 1:
        pairs = [a + b for a, b in zip(terms[::2], terms[1::2])]
        terms = pairs + terms[len(terms) // 2 * 2 :]
    return terms[0]


def invert_pairs(mat):
    tile = 8
    inner = iota((tile, LANES), 1) % GROUP_SLOTS
    base = iota((tile, LANES), 1) - inner
    sub = iota((tile, LANES), 0)
    parts = [mat[i : i + tile] for i in range(0, GROUP_SLOTS, tile)]

    def line_of(part, line):
        return jnp.broadcast_to(part[line : line + 1], (tile, LANES))

    for home in range(len(parts)):
        start = home * tile
        rows = parts[home]
        spread = [line_of(rows, k) for k in range(tile)]
        ahead = [jnp.take_along_axis(line, base + start + sub, axis=1) for line in spread]
        columns = [None] * len(parts)
        for i in [(home + 1 + q) % len(parts) for q in range(len(parts) - 1)]:
            columns[i] = [jnp.take_along_axis(line, base + tile * i + sub, axis=1) for line in spread]
        columns[home] = ahead
        ahead = list(ahead)
        for j in range(0, tile, 2):
            first, second = ahead[j], ahead[j + 1]
            p00, p01, p11 = line_of(first, j), line_of(second, j), line_of(second, j + 1)
            scale = 1.0 / (p00 * p11 - p01 * p01)
            lines = sub // 2 == j // 2
            first = jnp.where(sub == j, -1.0, jnp.where(sub == j + 1, 0.0, first))
            second = jnp.where(sub == j + 1, -1.0, jnp.where(sub == j, 0.0, second))

            def reduced(kept, upper, lower):
                above, below = p11 * upper - p01 * lower, p00 * lower - p01 * upper
                return kept - (first * above + second * below) * scale

            for k in range(j + 2, tile):
                kept = jnp.where(lines, 0.0, ahead[k])
                ahead[k] = reduced(kept, line_of(ahead[k], j), line_of(ahead[k], j + 1))
            here, there = inner == start + j, inner == start + j + 1
            kept = jnp.where(lines | here | there, 0.0, rows)
            upper = jnp.where(here, 1.0, jnp.where(there, 0.0, line_of(rows, j)))
            lower = jnp.where(there, 1.0, jnp.where(here, 0.0, line_of(rows, j + 1)))
            rows = reduced(kept, upper, lower)
        lines = [line_of(rows, k) for k in range(tile)]
        within = inner // tile == home
        for i in [(home + 1 + q) % len(parts) for q in range(len(parts) - 1)]:
            change = total_of([a * b for a, b in zip(columns[i], lines)])
            kept = jnp.where(within, 0.0, parts[i])
            parts[i] = kept - change if i > home else kept + change
        parts[home] = rows
    return jnp.concatenate(parts, axis=0)


def fused_kernel(
    n, sc_count, users, tau_count, antennas, gram_scale, estimate_scale,
    pilot_ref, data_ref, large_ref, pilot_index_ref, serving_ref, group_ref,
    out_ref,
    pilots, data, large_in, pilot_index, serving_in, group_in,
    grams, terms, term_recv,
    load, halo_send, halo_recv, gram_send, gram_arrive, given_send, given_arrive, out_send, out_recv, ready, side,
):
    me = lax.axis_index("ap")
    sc = lax.axis_index("sc")
    right, left = sc + 1, sc - 1
    pilot_rows = tau_count * antennas
    small = users - GROUP_SLOTS
    out_rows = n // 4 * GROUP_SLOTS // n

    loads = []
    for source, target in (
        (group_ref, group_in), (pilot_index_ref, pilot_index), (large_ref, large_in),
        (pilot_ref, pilots.at[pl.ds(pilot_rows, pilot_rows)]), (serving_ref, serving_in), (data_ref, data),
    ):
        loads.append(pltpu.make_async_copy(source, target, load.at[len(loads)]))
        loads[-1].start()

    def signal(semaphore, **where):
        pl.semaphore_signal(semaphore, inc=1, device_id=where, device_id_type=pl.DeviceIdType.MESH)

    barrier = pltpu.get_barrier_semaphore()
    has_left, has_right = sc > 0, sc < sc_count - 1
    pl.when(has_right)(functools.partial(signal, barrier, sc=right))

    anchors = jnp.where(has_left, 0, n)
    anchor = me < anchors
    giver, taker = anchor & (me == 0), anchor & (me == 1)
    hubbed = sc == sc_count - 2
    is_hub = (me == n // 2) & (sc == sc_count - 1)
    pl.when(hubbed)(functools.partial(signal, barrier, ap=n // 2, sc=right))

    @pl.loop(jnp.where(hubbed, n, me + 1), n)
    def _(peer):
        signal(barrier, ap=peer)

    @pl.loop(jnp.where(me > 1, 1, 0), jnp.minimum(anchors, me))
    def _(peer):
        signal(barrier, ap=peer)


    def make(src, dst, send_sem, recv_sem, where):
        return pltpu.make_async_remote_copy(
            src_ref=src, dst_ref=dst, send_sem=send_sem, recv_sem=recv_sem,
            device_id=where, device_id_type=pl.DeviceIdType.MESH,
        )

    middle = pilots.at[pl.ds(pilot_rows, pilot_rows)]
    first, last = (pilots.at[pl.ds(i * pilot_rows, pilot_rows)] for i in (0, 2))
    upward = make(middle, first, halo_send.at[0], halo_recv.at[0], {"sc": right})
    downward = make(pilot_ref, last, halo_send.at[1], halo_recv.at[1], {"sc": left})

    def enter():
        peers = jnp.where(anchor, jnp.where(giver, 1, n - 1), jnp.where(hubbed, 0, me)) + jnp.where(is_hub, n, 0)
        pl.semaphore_wait(barrier, has_left.astype(jnp.int32) + peers)
        pl.when(has_left)(functools.partial(signal, side, sc=left))
        pl.when(has_left)(downward.start)

        @pl.loop(jnp.where(hubbed, me, anchors), me)
        def _(peer):
            signal(ready.at[me], ap=peer)

        @pl.loop(0, jnp.where(is_hub, n, 0))
        def _(peer):
            signal(ready.at[0], ap=peer, sc=left)

    pl.when(jnp.logical_not(anchor))(enter)
    @pl.when(anchor & (me > 1))
    def _():
        grams[0] = jnp.zeros(grams.shape[1:], F32)

    blank = jnp.zeros((pilot_rows, pilots.shape[1]), BF16)

    @pl.when(jnp.logical_not(has_left))
    def _():
        pilots[pl.ds(0, pilot_rows), :] = blank

    @pl.when(jnp.logical_not(has_right))
    def _():
        pilots[pl.ds(2 * pilot_rows, pilot_rows), :] = blank

    for copy in loads[:3]:
        copy.wait()
    group = group_in[...]
    wide = (users, 2 * LANES)
    earlier = jnp.where((iota(wide, 0) < iota(wide, 1)) | (iota(wide, 1) >= LANES), 1.0, 0.0)
    counts = mm(jnp.broadcast_to(group, (8, users)).astype(F32).astype(BF16), earlier.astype(BF16))
    later_group = counts[:1, :users].astype(jnp.int32)
    second_large = counts[:1, LANES:] > GROUP_SLOTS - 0.5
    rank = jnp.where(group == 1, later_group, iota(group.shape, 1) - later_group)
    is_large = (group == 1) == second_large[:, :users]
    slot_row = jnp.where(is_large, rank, rank + GROUP_SLOTS)
    hot = jnp.where(iota((users, users), 0) == slot_row, 1.0, 0.0).astype(BF16)
    tall = (LANES, users)
    facts = jnp.concatenate(
        [jnp.broadcast_to(pilot_index[...], tall).astype(F32), iota(tall, 1).astype(F32)], axis=0
    )
    facts = mm(hot, facts.astype(BF16), NT)
    slot_pilot, member = facts[:, :LANES].astype(jnp.int32), facts[:, LANES:].astype(jnp.int32)
    same_pilot = jnp.where(slot_pilot[:, :users] == pilot_index[...], 1.0, 0.0).astype(BF16)
    large = large_in[...]
    contamination = 1.0 + tau_count / users * mm(same_pilot, large)
    coeff = mm(hot, large) * lax.rsqrt(contamination)

    low = jnp.where(sc == 0, 0.0, 0.25)
    high = jnp.where(sc == sc_count - 1, 0.0, 0.25)
    lane = iota((users, LANES), 1)
    meets = slot_pilot == lane % pilot_rows // antennas
    early = jnp.where(meets, jnp.where(lane < pilot_rows, low, 1.0 - low - high), 0.0)
    late = jnp.where(meets, high, 0.0)
    spread = jnp.concatenate(
        [
            jnp.concatenate(
                [
                    jnp.where(lane % antennas == a, early, 0.0).astype(BF16),
                    jnp.where(lane % antennas == a, late, 0.0).astype(BF16)[:, :pilot_rows],
                ],
                axis=1,
            )
            for a in range(antennas)
        ],
        axis=0,
    )

    loads[3].wait()

    @pl.when(has_right)
    def _():
        pl.semaphore_wait(side, 1)
        upward.start()

    pl.when(has_left)(upward.wait_recv)
    pl.when(has_right)(downward.wait_recv)
    smooth = mm(spread, pilots[...])
    channel = jnp.concatenate(
        [(smooth[a * users : (a + 1) * users] * coeff).astype(BF16) for a in range(antennas)], axis=1
    )
    channel = jnp.concatenate([channel, jnp.zeros((LANES - users, channel.shape[1]), BF16)], axis=0)
    gram = mm(channel[:users], channel, NT) * gram_scale

    def turn(part, amount):
        return pltpu.roll(part, amount % LANES, 1)

    lane, row = iota((small, LANES), 1), iota((small, LANES), 0)
    top, bottom, other = (gram[i * small : (i + 1) * small] for i in range(3))
    packed = jnp.where(lane < row, turn(bottom, -small), jnp.where(lane < GROUP_SLOTS, top, other))
    last = packed[small - 8 :]
    eight = iota((8, LANES), 1)
    for i in range(3):
        grams[me, pl.ds(8 * i, 8), :] = jnp.where(
            eight < users, packed[8 * i : 8 * i + 8], turn(last, users - small * i)
        )
    diagonal = [
        jnp.where(lane == row + i * small, part, 0.0) for i, part in enumerate((top, bottom, other))
    ]
    gram_rows = small - 7
    grams[me, pl.ds(gram_rows - 1, 1), :] = jnp.sum(total_of(diagonal), axis=0, keepdims=True)
    own = grams.at[me, pl.ds(0, gram_rows)]
    pl.when(anchor)(enter)
    given = grams.at[0, pl.ds(0, gram_rows)]
    gift = make(given, given, given_send, given_arrive, {"ap": 1})
    pl.when(giver)(gift.start)

    @pl.when(taker)
    def _():
        gift.wait_recv()
        grams[1, pl.ds(0, gram_rows), :] += grams[0, pl.ds(0, gram_rows), :]

    @pl.when(hubbed)
    def _():
        pl.semaphore_wait(ready.at[0], 1)

    known = anchor | hubbed

    @pl.loop(0, jnp.where(giver, 0, n - 1))
    def _(i):
        down = n - 1 - i
        peer = jnp.where(known, jnp.where(down > me, down, down - 1), jnp.where(i < me, i, i + 1))

        @pl.when(jnp.logical_not(known) & (peer > me))
        def _():
            pl.semaphore_wait(ready.at[peer], 1)

        make(own, own, gram_send, gram_arrive, {"ap": peer}).start()

    for copy in loads[4:]:
        copy.wait()
    serving = serving_in[...]
    mask = jnp.zeros((users, serving.shape[1]), F32)
    for j in range(serving.shape[0]):
        mask = jnp.where(member == serving[j : j + 1, :], 1.0, mask)
    mask = mask.astype(BF16)

    every = grams.at[pl.ds(0, n - 1), pl.ds(0, gram_rows)]
    fewer = grams.at[pl.ds(0, n - 2), pl.ds(0, gram_rows)]
    direct = jnp.logical_not(anchor) | giver
    pl.when(direct)(pltpu.make_async_copy(every, every, gram_arrive).wait)
    pl.when(jnp.logical_not(direct))(pltpu.make_async_copy(fewer, fewer, gram_arrive).wait)
    total = [grams[i, pl.ds(0, gram_rows), :] for i in range(n)]
    total = total_of([jnp.where(anchor, 0.0, total[0])] + total[1:])
    parts = [total[8 * i : 8 * i + 8] for i in range(3)]
    last = jnp.where(eight < 2 * small, turn(parts[1], small - users), turn(parts[2], 2 * small - users))
    last = jnp.where(eight < small, turn(parts[0], -users), last)
    packed = jnp.concatenate(parts + [last], axis=0)
    shifted, shifted_twice = turn(packed, small), turn(packed, 2 * small)
    mirrored = jnp.transpose(jnp.concatenate([packed, shifted, shifted_twice, shifted_twice], axis=0))
    within = lane % GROUP_SLOTS >= row
    upper = jnp.where(within, packed, mirrored[:small])
    upper = jnp.where(lane < users, upper, 0.0)
    lower = jnp.where((lane >= small) & (lane - small < row), shifted, mirrored[small : 2 * small])
    lower = jnp.where(lane < GROUP_SLOTS, lower, 0.0)
    system = jnp.concatenate([upper, lower], axis=0)
    lane, row = iota(system.shape, 1), iota(system.shape, 0)
    system = jnp.where(lane % GROUP_SLOTS == row, total[gram_rows - 1 : gram_rows] + NOISE_LEVEL, system)
    inverse = invert_pairs(system)
    weights = jnp.concatenate(
        [
            jnp.where(lane < GROUP_SLOTS, inverse, 0.0),
            jnp.where((lane >= GROUP_SLOTS) & (lane < users), inverse, 0.0)[:small],
        ],
        axis=0,
    ).astype(BF16)
    combine = mm(weights, channel).astype(BF16)
    masked = combine * jnp.concatenate([mask] * antennas, axis=1)
    found = mm(masked, data[...]) * estimate_scale
    large_group = found[:GROUP_SLOTS]
    small_group = jnp.concatenate([found[GROUP_SLOTS:], jnp.zeros((GROUP_SLOTS - small, LANES), F32)], axis=0)
    terms[pl.ds(0, GROUP_SLOTS), :] = jnp.where(second_large, small_group, large_group)
    terms[pl.ds(GROUP_SLOTS, GROUP_SLOTS), :] = jnp.where(second_large, large_group, small_group)

    def give(peer):
        make(
            terms.at[pl.ds(peer * out_rows, out_rows)], term_recv.at[me], out_send, out_recv, {"ap": peer}
        ).start()

    pl.loop(0, me)(give)
    pl.loop(me + 1, n)(lambda i: give(n + me - i))
    term_recv[me] = terms[pl.ds(me * out_rows, out_rows), :]
    shares = term_recv.at[pl.ds(0, n - 1)]
    pltpu.make_async_copy(shares, shares, out_recv).wait()
    out_ref[...] = total_of([term_recv[i] for i in range(n)])
    pl.when(giver)(gift.wait_send)
    pl.when(jnp.logical_not(giver))(pltpu.make_async_copy(every, every, gram_send).wait)
    pltpu.make_async_copy(shares, shares, out_send).wait()
    pl.when(has_right)(upward.wait_send)
    pl.when(has_left)(downward.wait_send)


def fused(pilot_received, received, large_scale, pilot_index, serving, user_group):
    n = lax.axis_size("ap")
    sc_count = lax.axis_size("sc")
    _, tau_count, antennas, aps_dev = pilot_received.shape
    symbols = received.shape[3]
    users = pilot_index.shape[0]
    slots = n // 4 * GROUP_SLOTS
    pilot_rows = tau_count * antennas
    out_rows = slots // n
    aps_total = aps_dev * n
    gram_scale = 1.0 / (antennas * aps_total)
    estimate_scale = 1.0 / math.sqrt(antennas * aps_total * serving.shape[1] / users)
    vmem = pl.BlockSpec(memory_space=pltpu.VMEM)
    two = pltpu.SemaphoreType.DMA((2,))
    one = pltpu.SemaphoreType.DMA
    out = pl.pallas_call(
        functools.partial(
            fused_kernel, n, sc_count, users, tau_count, antennas, gram_scale, estimate_scale
        ),
        out_shape=pltpu.VMEM((out_rows, symbols), F32),
        in_specs=[pl.BlockSpec(memory_space=pl.ANY)] * 6,
        out_specs=vmem,
        scratch_shapes=[
            pltpu.VMEM((3 * pilot_rows, aps_dev), BF16),
            pltpu.VMEM((antennas * aps_dev, symbols), BF16),
            pltpu.VMEM((users, aps_dev), BF16),
            pltpu.VMEM((1, users), jnp.int32),
            pltpu.VMEM((serving.shape[1], aps_dev), jnp.int32),
            pltpu.VMEM((1, users), jnp.int32),
            pltpu.VMEM((n, GROUP_SLOTS // 2, LANES), F32),
            pltpu.VMEM((slots, symbols), F32),
            pltpu.VMEM((n, out_rows, symbols), F32),
            pltpu.SemaphoreType.DMA((6,)),
            two, two, one, one, one, one, one, one, pltpu.SemaphoreType.REGULAR((n,)), pltpu.SemaphoreType.REGULAR,
        ],
        compiler_params=pltpu.CompilerParams(collective_id=0, has_side_effects=True),
    )(
        pilot_received.reshape(pilot_rows, aps_dev),
        received.reshape(antennas * aps_dev, symbols),
        large_scale,
        pilot_index.reshape(1, users),
        serving.T,
        user_group.reshape(1, users),
    )
    return out.reshape(out_rows, 1, symbols)


def solution(mesh):
    in_specs = (
        P("sc", None, None, "ap"),
        P("sc", None, "ap", None),
        P(None, "ap"),
        P(),
        P("ap", None),
        P(),
    )
    out_specs = P("ap", "sc", None)

    def per_device(*arguments):
        slots = mesh.shape["ap"] // 4 * GROUP_SLOTS
        users = arguments[3].shape[0]
        filled = slots == LANES and 4 * users == 3 * slots and mesh.shape["sc"] > 2
        return (fused if filled else on_device)(*arguments)

    return jax.shard_map(
        per_device, mesh=mesh, in_specs=in_specs, out_specs=out_specs, check_vma=False
    )
```

```python
import functools
import math

import jax
import jax.numpy as jnp
from jax import lax
from jax.experimental import pallas as pl
from jax.experimental.pallas import tpu as pltpu
from jax.sharding import PartitionSpec as P

GROUP_SLOTS = 64


NOISE_LEVEL = 0.05


def extended_2(block, sides, width):
    for axis, dim in sides:
        count = lax.axis_size(axis)
        forward = [(i, i + 1) for i in range(count - 1)]
        backward = [(target, source) for source, target in forward]
        low = lax.ppermute(
            lax.slice_in_dim(block, block.shape[dim] - width, None, axis=dim), axis, forward
        )
        high = lax.ppermute(lax.slice_in_dim(block, 0, width, axis=dim), axis, backward)
        block = jnp.concatenate([low, block, high], axis=dim)
    return block


def slot_tables(pilot_index, user_group, group_count):
    labels = jnp.arange(group_count, dtype=jnp.int32)
    group_hot = (user_group[:, None] == labels[None, :]).astype(jnp.int32)
    users = jnp.arange(user_group.shape[0], dtype=jnp.int32)
    up_to = (users[:, None] >= users[None, :]).astype(jnp.bfloat16)
    counts = jnp.dot(up_to, group_hot.astype(jnp.bfloat16), preferred_element_type=jnp.float32)
    ranks_in = jnp.sum(counts.astype(jnp.int32) * group_hot, axis=1) - 1
    slot_ids = user_group * GROUP_SLOTS + ranks_in
    members = (
        jnp.zeros((group_count * GROUP_SLOTS,), jnp.int32)
        .at[slot_ids]
        .set(jnp.arange(user_group.shape[0], dtype=jnp.int32))
    )
    occupied = jnp.zeros((group_count * GROUP_SLOTS,), jnp.float32).at[slot_ids].set(1.0)
    slot_pilot = pilot_index[members]
    return (members, occupied, slot_pilot)


def inverse_columns(factor, columns):
    first = lax.linalg.triangular_solve(factor, columns, left_side=True, lower=True)
    return lax.linalg.triangular_solve(factor, first, left_side=True, lower=True, transpose_a=True)


def on_device(pilot_received, received, large_scale, pilot_index, serving, user_group):
    ap_count = lax.axis_size("ap")
    sc_count = lax.axis_size("sc")
    ap_index = lax.axis_index("ap")
    sc_index = lax.axis_index("sc")
    blocks_dev, tau_count, antennas, aps_dev = pilot_received.shape
    symbols = received.shape[3]
    users = pilot_index.shape[0]
    serve_count = serving.shape[1]
    groups = ap_count // 4
    quarter = GROUP_SLOTS // 4
    aps_total = aps_dev * ap_count
    members, occupied, slot_pilot = slot_tables(pilot_index, user_group, groups)
    extended = extended_2(pilot_received, (("sc", 0),), 1)
    block_ids = sc_index * blocks_dev + jnp.arange(blocks_dev, dtype=jnp.int32)
    first_block = (block_ids == 0)[:, None, None, None]
    final_block = (block_ids == blocks_dev * sc_count - 1)[:, None, None, None]
    middle = extended[1:-1].astype(jnp.float32)
    before = jnp.where(first_block, middle, extended[:-2].astype(jnp.float32))
    after = jnp.where(final_block, middle, extended[2:].astype(jnp.float32))
    smooth = 0.25 * before + 0.5 * middle + 0.25 * after
    pilot_hot = (pilot_index[None, :] == jnp.arange(tau_count, dtype=jnp.int32)[:, None]).astype(
        jnp.bfloat16
    )
    contamination = 1.0 + tau_count / users * jnp.dot(
        pilot_hot, large_scale, preferred_element_type=jnp.float32
    )
    serve_mask = (
        jnp.zeros((users, aps_dev), jnp.bfloat16)
        .at[serving, jnp.arange(aps_dev, dtype=jnp.int32)[:, None]]
        .set(1.0)
    )
    batch_groups = min(8, groups)
    batches = groups // batch_groups
    batch_rows = batch_groups * GROUP_SLOTS
    member_blocks = members.reshape(batches, batch_rows)
    occupied_blocks = occupied.reshape(batches, batch_rows)
    pilot_blocks = slot_pilot.reshape(batches, batch_rows)
    gramian_scale = 1.0 / (antennas * aps_total)

    def gram_batch(inputs):
        member_rows, occupied_rows, pilot_rows = inputs
        coeff = (
            occupied_rows[:, None]
            * large_scale[member_rows].astype(jnp.float32)
            * lax.rsqrt(contamination[pilot_rows])
        )
        row_hot = (pilot_rows[:, None] == jnp.arange(tau_count, dtype=jnp.int32)).astype(jnp.float32)
        picked = jnp.einsum("st,btnl->bsnl", row_hot, smooth, precision=lax.Precision.HIGHEST)
        channel_gain = (picked * coeff[None, :, None, :]).astype(jnp.bfloat16)
        channel_gain = channel_gain.reshape(
            blocks_dev, batch_groups, GROUP_SLOTS, antennas * aps_dev
        )
        gram = (
            jnp.einsum(
                "bogx,bohx->ogbh", channel_gain, channel_gain, preferred_element_type=jnp.float32
            )
            * gramian_scale
        )
        return (gram, channel_gain)

    partial_gram, channel_store = lax.map(
        gram_batch, (member_blocks, occupied_blocks, pilot_blocks)
    )
    partial_gram = partial_gram.reshape(groups * GROUP_SLOTS, blocks_dev, GROUP_SLOTS)
    summed = lax.psum(partial_gram, "ap")
    owned = lax.dynamic_slice_in_dim(summed, ap_index // 4 * GROUP_SLOTS, GROUP_SLOTS, 0)
    identity = jnp.eye(GROUP_SLOTS, dtype=jnp.float32)
    system = jnp.transpose(owned, (1, 0, 2)) + NOISE_LEVEL * identity
    factor = jnp.linalg.cholesky(system)
    columns = lax.dynamic_slice_in_dim(identity, ap_index % 4 * quarter, quarter, 1)
    solved = inverse_columns(factor, jnp.broadcast_to(columns, (blocks_dev, GROUP_SLOTS, quarter)))
    weight_rows = jnp.transpose(solved, (2, 0, 1)).astype(jnp.bfloat16)
    all_weights = lax.all_gather(weight_rows, "ap", axis=0, tiled=True)
    weight_blocks = all_weights.reshape(batches, batch_groups, GROUP_SLOTS, blocks_dev, GROUP_SLOTS)
    data_signal = received.reshape(blocks_dev, antennas * aps_dev, symbols)
    estimator_scale = 1.0 / math.sqrt(antennas * aps_total * serve_count / users)

    def estimate_batch(inputs):
        member_rows, occupied_rows, channel_gain, weights = inputs
        combiner_weight = jnp.einsum(
            "okbj,bojx->bokx", weights, channel_gain, preferred_element_type=jnp.float32
        ).astype(jnp.bfloat16)
        row_mask_values = serve_mask[member_rows] * occupied_rows[:, None].astype(jnp.bfloat16)
        masked_values = (
            combiner_weight.reshape(blocks_dev, batch_rows, antennas, aps_dev)
            * row_mask_values[None, :, None, :]
        )
        flattened_masked = masked_values.reshape(blocks_dev, batch_rows, antennas * aps_dev)
        return (
            jnp.einsum(
                "bsx,bxt->sbt", flattened_masked, data_signal, preferred_element_type=jnp.float32
            )
            * estimator_scale
        )

    terms = lax.map(estimate_batch, (member_blocks, occupied_blocks, channel_store, weight_blocks))
    terms = terms.reshape(groups * GROUP_SLOTS, blocks_dev, symbols)
    return lax.psum_scatter(terms, "ap", scatter_dimension=0, tiled=True)


LANES = 128
BF16 = jnp.bfloat16
F32 = jnp.float32
NT = (((1,), (1,)), ((), ()))


def iota(shape, dim):
    return lax.broadcasted_iota(jnp.int32, shape, dim)


def mm(a, b, dims=(((1,), (0,)), ((), ()))):
    return lax.dot_general(a, b, dims, preferred_element_type=F32)


def total_of(terms):
    while len(terms) > 1:
        pairs = [a + b for a, b in zip(terms[::2], terms[1::2])]
        terms = pairs + terms[len(terms) // 2 * 2 :]
    return terms[0]


def invert_pairs(parts):
    tile = 8
    inner = iota((tile, LANES), 1) % GROUP_SLOTS
    base = iota((tile, LANES), 1) - inner
    sub = iota((tile, LANES), 0)
    parts = list(parts)

    def line_of(part, line):
        return jnp.broadcast_to(part[line : line + 1], (tile, LANES))

    for home in range(len(parts)):
        start = home * tile
        rows = parts[home]
        spread = [line_of(rows, k) for k in range(tile)]
        ahead = [jnp.take_along_axis(line, base + start + sub, axis=1) for line in spread]
        columns = [None] * len(parts)
        for i in [(home + 1 + q) % len(parts) for q in range(len(parts) - 1)]:
            columns[i] = [jnp.take_along_axis(line, base + tile * i + sub, axis=1) for line in spread]
        columns[home] = ahead
        ahead = list(ahead)
        for j in range(0, tile, 2):
            first, second = ahead[j], ahead[j + 1]
            p00, p01, p11 = line_of(first, j), line_of(second, j), line_of(second, j + 1)
            scale = 1.0 / (p00 * p11 - p01 * p01)
            lines = sub // 2 == j // 2
            first = jnp.where(sub == j, -1.0, jnp.where(sub == j + 1, 0.0, first))
            second = jnp.where(sub == j + 1, -1.0, jnp.where(sub == j, 0.0, second))

            def reduced(kept, upper, lower):
                above, below = p11 * upper - p01 * lower, p00 * lower - p01 * upper
                return kept - (first * above + second * below) * scale

            for k in range(j + 2, tile):
                kept = jnp.where(lines, 0.0, ahead[k])
                ahead[k] = reduced(kept, line_of(ahead[k], j), line_of(ahead[k], j + 1))
            here, there = inner == start + j, inner == start + j + 1
            kept = jnp.where(lines | here | there, 0.0, rows)
            upper = jnp.where(here, 1.0, jnp.where(there, 0.0, line_of(rows, j)))
            lower = jnp.where(there, 1.0, jnp.where(here, 0.0, line_of(rows, j + 1)))
            rows = reduced(kept, upper, lower)
        lines = [line_of(rows, k) for k in range(tile)]
        within = inner // tile == home
        for i in [(home + 1 + q) % len(parts) for q in range(len(parts) - 1)]:
            change = total_of([a * b for a, b in zip(columns[i], lines)])
            kept = jnp.where(within, 0.0, parts[i])
            parts[i] = kept - change if i > home else kept + change
        parts[home] = rows
    return jnp.concatenate(parts, axis=0)


def fused_kernel(
    n, sc_count, users, tau_count, antennas, gram_scale, estimate_scale,
    pilot_ref, data_ref, large_ref, pilot_index_ref, serving_ref, group_ref,
    out_ref,
    pilots, data, large_in, pilot_index, serving_in, group_in,
    grams, terms, term_recv,
    load, halo_send, halo_recv, gram_send, gram_arrive, given_send, given_arrive, out_send, out_recv, ready, side,
):
    me = lax.axis_index("ap")
    sc = lax.axis_index("sc")
    right, left = sc + 1, sc - 1
    pilot_rows = tau_count * antennas
    small = users - GROUP_SLOTS
    out_rows = n // 4 * GROUP_SLOTS // n

    loads = []
    for source, target in (
        (group_ref, group_in), (pilot_index_ref, pilot_index), (large_ref, large_in),
        (pilot_ref, pilots.at[pl.ds(pilot_rows, pilot_rows)]), (serving_ref, serving_in), (data_ref, data),
    ):
        loads.append(pltpu.make_async_copy(source, target, load.at[len(loads)]))
        loads[-1].start()

    def signal(semaphore, **where):
        pl.semaphore_signal(semaphore, inc=1, device_id=where, device_id_type=pl.DeviceIdType.MESH)

    barrier = pltpu.get_barrier_semaphore()
    has_left, has_right = sc > 0, sc < sc_count - 1
    pl.when(has_right)(functools.partial(signal, barrier, sc=right))

    anchors = jnp.where(has_left, 0, n)
    anchor = me < anchors
    giver, taker = anchor & (me == 0), anchor & (me == 1)
    hubbed = sc == sc_count - 2
    is_hub = (me == n // 2) & (sc == sc_count - 1)
    pl.when(hubbed)(functools.partial(signal, barrier, ap=n // 2, sc=right))

    @pl.loop(jnp.where(hubbed, n, me + 1), n)
    def _(peer):
        signal(barrier, ap=peer)

    @pl.loop(jnp.where(me > 1, 1, 0), jnp.minimum(anchors, me))
    def _(peer):
        signal(barrier, ap=peer)


    def make(src, dst, send_sem, recv_sem, where):
        return pltpu.make_async_remote_copy(
            src_ref=src, dst_ref=dst, send_sem=send_sem, recv_sem=recv_sem,
            device_id=where, device_id_type=pl.DeviceIdType.MESH,
        )

    middle = pilots.at[pl.ds(pilot_rows, pilot_rows)]
    first, last = (pilots.at[pl.ds(i * pilot_rows, pilot_rows)] for i in (0, 2))
    upward = make(middle, first, halo_send.at[0], halo_recv.at[0], {"sc": right})
    downward = make(pilot_ref, last, halo_send.at[1], halo_recv.at[1], {"sc": left})

    def enter():
        peers = jnp.where(anchor, jnp.where(giver, 1, n - 1), jnp.where(hubbed, 0, me)) + jnp.where(is_hub, n, 0)
        pl.semaphore_wait(barrier, has_left.astype(jnp.int32) + peers)
        pl.when(has_left)(functools.partial(signal, side, sc=left))
        pl.when(has_left)(downward.start)

        @pl.loop(jnp.where(hubbed, me, anchors), me)
        def _(peer):
            signal(ready.at[me], ap=peer)

        @pl.loop(0, jnp.where(is_hub, n, 0))
        def _(peer):
            signal(ready.at[0], ap=peer, sc=left)

    pl.when(jnp.logical_not(anchor))(enter)
    @pl.when(anchor & (me > 1))
    def _():
        grams[0] = jnp.zeros(grams.shape[1:], F32)

    blank = jnp.zeros((pilot_rows, pilots.shape[1]), BF16)

    @pl.when(jnp.logical_not(has_left))
    def _():
        pilots[pl.ds(0, pilot_rows), :] = blank

    @pl.when(jnp.logical_not(has_right))
    def _():
        pilots[pl.ds(2 * pilot_rows, pilot_rows), :] = blank

    for copy in loads[:3]:
        copy.wait()
    group = group_in[...]
    wide = (users, 2 * LANES)
    earlier = jnp.where((iota(wide, 0) < iota(wide, 1)) | (iota(wide, 1) >= LANES), 1.0, 0.0)
    counts = mm(jnp.broadcast_to(group, (8, users)).astype(F32).astype(BF16), earlier.astype(BF16))
    later_group = counts[:1, :users].astype(jnp.int32)
    second_large = counts[:1, LANES:] > GROUP_SLOTS - 0.5
    rank = jnp.where(group == 1, later_group, iota(group.shape, 1) - later_group)
    is_large = (group == 1) == second_large[:, :users]
    slot_row = jnp.where(is_large, rank, rank + GROUP_SLOTS)
    hot = jnp.where(iota((users, users), 0) == slot_row, 1.0, 0.0).astype(BF16)
    tall = (LANES, users)
    facts = jnp.concatenate(
        [jnp.broadcast_to(pilot_index[...], tall).astype(F32), iota(tall, 1).astype(F32)], axis=0
    )
    facts = mm(hot, facts.astype(BF16), NT)
    slot_pilot, member = facts[:, :LANES].astype(jnp.int32), facts[:, LANES:].astype(jnp.int32)
    same_pilot = jnp.where(slot_pilot[:, :users] == pilot_index[...], 1.0, 0.0).astype(BF16)
    large = large_in[...]
    contamination = 1.0 + tau_count / users * mm(same_pilot, large)
    coeff = mm(hot, large) * lax.rsqrt(contamination)

    low = jnp.where(sc == 0, 0.0, 0.25)
    high = jnp.where(sc == sc_count - 1, 0.0, 0.25)
    lane = iota((users, LANES), 1)
    meets = slot_pilot == lane % pilot_rows // antennas
    early = jnp.where(meets, jnp.where(lane < pilot_rows, low, 1.0 - low - high), 0.0)
    late = jnp.where(meets, high, 0.0)
    spread = jnp.concatenate(
        [
            jnp.concatenate(
                [
                    jnp.where(lane % antennas == a, early, 0.0).astype(BF16),
                    jnp.where(lane % antennas == a, late, 0.0).astype(BF16)[:, :pilot_rows],
                ],
                axis=1,
            )
            for a in range(antennas)
        ],
        axis=0,
    )

    loads[3].wait()

    @pl.when(has_right)
    def _():
        pl.semaphore_wait(side, 1)
        upward.start()

    pl.when(has_left)(upward.wait_recv)
    pl.when(has_right)(downward.wait_recv)
    smooth = mm(spread, pilots[...])
    channel = jnp.concatenate(
        [(smooth[a * users : (a + 1) * users] * coeff).astype(BF16) for a in range(antennas)], axis=1
    )
    channel = jnp.concatenate([channel, jnp.zeros((LANES - users, channel.shape[1]), BF16)], axis=0)
    gram = mm(channel[:users], channel, NT) * gram_scale

    def turn(part, amount):
        return pltpu.roll(part, amount % LANES, 1)

    eight = iota((8, LANES), 1)

    def lay(*pieces):
        *pieces, (_, whole) = pieces
        for end, piece in reversed(pieces):
            whole = jnp.where(eight < end, piece, whole)
        return whole

    b = [gram[i : i + 8] for i in range(0, users, 8)]
    gram_rows = 24
    grams[me, pl.ds(0, 8), :] = lay((64, b[0]), (120, turn(b[1], 56)), (LANES, turn(b[7], 64)))
    grams[me, pl.ds(8, 8), :] = lay(
        (16, turn(b[10], 48)), (64, b[2]), (88, turn(b[9], -8)), (LANES, turn(b[3], 64))
    )
    grams[me, pl.ds(16, 8), :] = lay(
        (16, turn(b[6], 80)), (32, turn(b[11], 56)), (64, b[4]), (96, b[8]), (LANES, turn(b[5], 64))
    )
    own = grams.at[me, pl.ds(0, gram_rows)]
    pl.when(anchor)(enter)
    given = grams.at[0, pl.ds(0, gram_rows)]
    gift = make(given, given, given_send, given_arrive, {"ap": 1})
    pl.when(giver)(gift.start)

    @pl.when(taker)
    def _():
        gift.wait_recv()
        grams[1, pl.ds(0, gram_rows), :] += grams[0, pl.ds(0, gram_rows), :]

    @pl.when(hubbed)
    def _():
        pl.semaphore_wait(ready.at[0], 1)

    known = anchor | hubbed

    @pl.loop(0, jnp.where(giver, 0, n - 1))
    def _(i):
        down = n - 1 - i
        peer = jnp.where(known, jnp.where(down > me, down, down - 1), jnp.where(i < me, i, i + 1))

        @pl.when(jnp.logical_not(known) & (peer > me))
        def _():
            pl.semaphore_wait(ready.at[peer], 1)

        make(own, own, gram_send, gram_arrive, {"ap": peer}).start()

    for copy in loads[4:]:
        copy.wait()
    serving = serving_in[...]
    mask = jnp.zeros((users, serving.shape[1]), F32)
    for j in range(serving.shape[0]):
        mask = jnp.where(member == serving[j : j + 1, :], 1.0, mask)
    mask = mask.astype(BF16)

    every = grams.at[pl.ds(0, n - 1), pl.ds(0, gram_rows)]
    fewer = grams.at[pl.ds(0, n - 2), pl.ds(0, gram_rows)]
    direct = jnp.logical_not(anchor) | giver
    pl.when(direct)(pltpu.make_async_copy(every, every, gram_arrive).wait)
    pl.when(jnp.logical_not(direct))(pltpu.make_async_copy(fewer, fewer, gram_arrive).wait)
    total = [grams[i, pl.ds(0, gram_rows), :] for i in range(n)]
    total = total_of([jnp.where(anchor, 0.0, total[0])] + total[1:])
    t0, t1, t2 = (total[i : i + 8] for i in range(0, gram_rows, 8))
    lefts = [t0, turn(t0, -56), t1, turn(t1, 64), t2, turn(t2, 64), turn(t2, 48), turn(t0, 64)]
    rights = [t2, turn(t1, 8), turn(t1, 80), turn(t2, 72)] + [0.0] * 4
    diagonal = eight % GROUP_SLOTS - iota((8, LANES), 0)
    system = [
        lay((GROUP_SLOTS, left), (users, right), (LANES, 0.0)) + jnp.where(diagonal == 8 * i, NOISE_LEVEL, 0.0)
        for i, (left, right) in enumerate(zip(lefts, rights))
    ]
    inverse = invert_pairs(system)
    lane = iota(inverse.shape, 1)
    weights = jnp.concatenate(
        [
            jnp.where(lane < GROUP_SLOTS, inverse, 0.0),
            jnp.where((lane >= GROUP_SLOTS) & (lane < users), inverse, 0.0)[:small],
        ],
        axis=0,
    ).astype(BF16)
    combine = mm(weights, channel).astype(BF16)
    masked = combine * jnp.concatenate([mask] * antennas, axis=1)
    found = mm(masked, data[...]) * estimate_scale
    large_group = found[:GROUP_SLOTS]
    small_group = jnp.concatenate([found[GROUP_SLOTS:], jnp.zeros((GROUP_SLOTS - small, LANES), F32)], axis=0)
    terms[pl.ds(0, GROUP_SLOTS), :] = jnp.where(second_large, small_group, large_group)
    terms[pl.ds(GROUP_SLOTS, GROUP_SLOTS), :] = jnp.where(second_large, large_group, small_group)

    def give(peer):
        make(
            terms.at[pl.ds(peer * out_rows, out_rows)], term_recv.at[me], out_send, out_recv, {"ap": peer}
        ).start()

    pl.loop(0, me)(give)
    pl.loop(me + 1, n)(lambda i: give(n + me - i))
    term_recv[me] = terms[pl.ds(me * out_rows, out_rows), :]
    shares = term_recv.at[pl.ds(0, n - 1)]
    pltpu.make_async_copy(shares, shares, out_recv).wait()
    out_ref[...] = total_of([term_recv[i] for i in range(n)])
    pl.when(giver)(gift.wait_send)
    pl.when(jnp.logical_not(giver))(pltpu.make_async_copy(every, every, gram_send).wait)
    pltpu.make_async_copy(shares, shares, out_send).wait()
    pl.when(has_right)(upward.wait_send)
    pl.when(has_left)(downward.wait_send)


def fused(pilot_received, received, large_scale, pilot_index, serving, user_group):
    n = lax.axis_size("ap")
    sc_count = lax.axis_size("sc")
    _, tau_count, antennas, aps_dev = pilot_received.shape
    symbols = received.shape[3]
    users = pilot_index.shape[0]
    slots = n // 4 * GROUP_SLOTS
    pilot_rows = tau_count * antennas
    out_rows = slots // n
    aps_total = aps_dev * n
    gram_scale = 1.0 / (antennas * aps_total)
    estimate_scale = 1.0 / math.sqrt(antennas * aps_total * serving.shape[1] / users)
    vmem = pl.BlockSpec(memory_space=pltpu.VMEM)
    two = pltpu.SemaphoreType.DMA((2,))
    one = pltpu.SemaphoreType.DMA
    out = pl.pallas_call(
        functools.partial(
            fused_kernel, n, sc_count, users, tau_count, antennas, gram_scale, estimate_scale
        ),
        out_shape=pltpu.VMEM((out_rows, symbols), F32),
        in_specs=[pl.BlockSpec(memory_space=pl.ANY)] * 6,
        out_specs=vmem,
        scratch_shapes=[
            pltpu.VMEM((3 * pilot_rows, aps_dev), BF16),
            pltpu.VMEM((antennas * aps_dev, symbols), BF16),
            pltpu.VMEM((users, aps_dev), BF16),
            pltpu.VMEM((1, users), jnp.int32),
            pltpu.VMEM((serving.shape[1], aps_dev), jnp.int32),
            pltpu.VMEM((1, users), jnp.int32),
            pltpu.VMEM((n, 24, LANES), F32),
            pltpu.VMEM((slots, symbols), F32),
            pltpu.VMEM((n, out_rows, symbols), F32),
            pltpu.SemaphoreType.DMA((6,)),
            two, two, one, one, one, one, one, one, pltpu.SemaphoreType.REGULAR((n,)), pltpu.SemaphoreType.REGULAR,
        ],
        compiler_params=pltpu.CompilerParams(collective_id=0, has_side_effects=True),
    )(
        pilot_received.reshape(pilot_rows, aps_dev),
        received.reshape(antennas * aps_dev, symbols),
        large_scale,
        pilot_index.reshape(1, users),
        serving.T,
        user_group.reshape(1, users),
    )
    return out.reshape(out_rows, 1, symbols)


def solution(mesh):
    in_specs = (
        P("sc", None, None, "ap"),
        P("sc", None, "ap", None),
        P(None, "ap"),
        P(),
        P("ap", None),
        P(),
    )
    out_specs = P("ap", "sc", None)

    def per_device(*arguments):
        slots = mesh.shape["ap"] // 4 * GROUP_SLOTS
        users = arguments[3].shape[0]
        filled = slots == LANES and 4 * users == 3 * slots and mesh.shape["sc"] > 2
        return (fused if filled else on_device)(*arguments)

    return jax.shard_map(
        per_device, mesh=mesh, in_specs=in_specs, out_specs=out_specs, check_vma=False
    )
```
